512 devices in a mesh: gx: 32 (over y, z_lo), gy: 16 (over x, z_hi, core).
Axes of the slice: x: 4, y: 4, z: 16 (z_hi: 2, z_lo: 8; z = z_hi * 8 + z_lo), core: 2. Of those that a mesh axis runs over, the one named last changes fastest.
Arguments:
- mass_per_volume: float32 [1024, 8192], P('gy', 'gx'), may hold values from 0.5 to 2
- motion_speed: float32 [1024, 3, 8192], P('gy', None, 'gx'), may hold values from -3 to 3
- agitation_energy: float32 [1024, 8192], P('gy', 'gx'), may hold values from 0.5 to 2
- shear_deviatoric: float32 [1024, 5, 8192], P('gy', None, 'gx'), may hold values from -2.4 to 2.4
- thermal_current_array: float32 [1024, 3, 8192], P('gy', None, 'gx'), may hold values from -2.4 to 2.4
Outputs:
- rate: float32 [1024, 13, 8192], P('gy', None, 'gx')
The draws below stay inside these ranges and needn't reach their ends.
All inputs are finite; a program needn't handle non-finite values.
Results may differ from the reference program's by a relative error of at most 0.0043.
The reference program's roundings to bfloat16 on the way (of `grid`) count: a program that leaves them out, or rounds other values in their place, can miss the bound.
Values may be sent and summed in bfloat16 or wider, within the bound.
A program may use at most 64 MiB of HBM per device.

```python
import math
import jax
import jax.numpy as jnp
from jax import lax

CROSS_NODES = 1024
DOWNFLOW_NODES = 8192


def block_scale(own_key, shape, split, low, top_value):
    def one(position, shards_of):
        heights = jax.random.uniform(jax.random.fold_in(jax.random.fold_in(own_key, 6), position), (shards_of,), jnp.float32, low / len(split), top_value / len(split))
        return jnp.repeat(jnp.exp(heights), shape[position] // shards_of).reshape((-1,) + (1,) * (len(shape) - position - 1))

    factor_of = one(*split[0])
    for cut in split[1:]:
        factor_of = factor_of * one(*cut)
    return factor_of


def gaussian(own_key, dims, scale, limit, cuts=(), held_as=jnp.bfloat16):
    drawn = scale * jax.random.normal(own_key, dims, jnp.float32)
    if cuts:
        drawn = drawn * block_scale(own_key, dims, cuts, -0.22, 0.18)
    return jnp.clip(drawn, -limit, limit).astype(held_as)


def setup_inputs(seed: int = 0) -> dict:
    streams_of = jax.random.split(jax.random.key(seed), 6)
    return {
        "mass_per_volume": jnp.clip(0.5 + 1.5 * jax.random.uniform(streams_of[0], (CROSS_NODES, DOWNFLOW_NODES), jnp.float32) ** block_scale(streams_of[0], (CROSS_NODES, DOWNFLOW_NODES), ((0, 16), (1, 32)), -0.2, 0.2), 0.5, 2.0),
        "motion_speed": gaussian(streams_of[1], (CROSS_NODES, 3, DOWNFLOW_NODES), 0.5, 3.0, ((0, 16), (2, 32)), jnp.float32),
        "agitation_energy": jnp.clip(0.5 + 1.5 * jax.random.uniform(streams_of[2], (CROSS_NODES, DOWNFLOW_NODES), jnp.float32) ** block_scale(streams_of[2], (CROSS_NODES, DOWNFLOW_NODES), ((0, 16), (1, 32)), -0.2, 0.2), 0.5, 2.0),
        "shear_deviatoric": gaussian(streams_of[3], (CROSS_NODES, 5, DOWNFLOW_NODES), 0.4, 2.4, ((0, 16), (2, 32)), jnp.float32),
        "thermal_current_array": gaussian(streams_of[4], (CROSS_NODES, 3, DOWNFLOW_NODES), 0.4, 2.4, ((0, 16), (2, 32)), jnp.float32),
    }


time_step = 0.05
enforcement_weight = 4.0
plate_speed = 0.5
dissipation_speed = 0.25

def derivative_rows(first, count, size):
    last = size - 1
    half = math.pi / (2.0 * last)
    rows = first + jnp.arange(count, dtype=jnp.int32)
    cols = jnp.arange(size, dtype=jnp.int32)
    summed = (rows[:, None] + cols[None, :]).astype(jnp.float32)
    differ = rows[:, None] - cols[None, :]
    same = differ == 0
    denom = -2.0 * jnp.sin(half * summed) * jnp.sin(half * differ.astype(jnp.float32))
    safe = jnp.where(same, jnp.float32(1.0), denom)

    def weights(index):
        edge = jnp.where((index == 0) | (index == last), jnp.float32(2.0), jnp.float32(1.0))
        parity = (1 - 2 * (index % 2)).astype(jnp.float32)
        return edge * parity
    ratio = weights(rows)[:, None] / weights(cols)[None, :]
    scale = math.pi / last * jnp.sin(2.0 * half * rows.astype(jnp.float32))
    offdiag = jnp.where(same, jnp.float32(0.0), scale[:, None] * ratio / safe)
    diagonal = -lax.optimization_barrier(jnp.sum(offdiag, axis=1))
    return (offdiag + jnp.where(same, diagonal[:, None], jnp.float32(0.0))).astype(jnp.bfloat16)

def fluxes(unknown_collection):
    agitation_energy = unknown_collection[:, 4]
    motion_speed = [unknown_collection[:, 1], unknown_collection[:, 2], unknown_collection[:, 3]]
    traction_matrix = [[unknown_collection[:, 5], unknown_collection[:, 6], unknown_collection[:, 8]], [unknown_collection[:, 6], unknown_collection[:, 7], unknown_collection[:, 9]], [unknown_collection[:, 8], unknown_collection[:, 9], -(unknown_collection[:, 5] + unknown_collection[:, 7])]]
    thermal_current_entry = [unknown_collection[:, 10], unknown_collection[:, 11], unknown_collection[:, 12]]
    pairs = [(0, 0), (0, 1), (1, 1), (0, 2), (1, 2)]
    result = []
    for spatial_axis_number in (0, 1):
        transported_quantity = motion_speed[spatial_axis_number]
        local_quantity = [unknown_collection[:, 0] * transported_quantity]
        for leading_subscript in range(3):
            local_quantity.append(motion_speed[leading_subscript] * transported_quantity + traction_matrix[leading_subscript][spatial_axis_number] + (agitation_energy if leading_subscript == spatial_axis_number else 0.0))
        local_quantity.append(transported_quantity * agitation_energy + 2.0 / 3.0 * thermal_current_entry[spatial_axis_number])
        for leading_subscript, trailing_subscript in pairs:
            production_entry = transported_quantity * traction_matrix[leading_subscript][trailing_subscript]
            production_entry = production_entry + 0.4 * ((thermal_current_entry[leading_subscript] if trailing_subscript == spatial_axis_number else 0.0) + (thermal_current_entry[trailing_subscript] if leading_subscript == spatial_axis_number else 0.0))
            production_entry = production_entry - (4.0 / 15.0 * thermal_current_entry[spatial_axis_number] if leading_subscript == trailing_subscript else 0.0)
            local_quantity.append(production_entry)
        for leading_subscript in range(3):
            local_quantity.append(transported_quantity * thermal_current_entry[leading_subscript] + agitation_energy * traction_matrix[leading_subscript][spatial_axis_number] + (2.5 * agitation_energy * agitation_energy if leading_subscript == spatial_axis_number else 0.0))
        result.append(jnp.stack(local_quantity, axis=1))
    return (result[0], result[1])

def source(unknown_collection, rows, size):
    mass_per_volume = unknown_collection[:, 0]
    agitation_energy = unknown_collection[:, 4]
    impact_often_measure = mass_per_volume * jnp.sqrt(agitation_energy * agitation_energy + 0.25)
    plate_condition = jnp.where(rows == 0, jnp.float32(1.0), jnp.where(rows == size - 1, jnp.float32(-1.0), jnp.float32(0.0)))[:, None]
    radial_distribution = jnp.abs(plate_condition)
    blank_quantity = jnp.zeros_like(mass_per_volume)
    production_entries = [blank_quantity, -enforcement_weight * radial_distribution * (unknown_collection[:, 1] - plate_speed * plate_condition), blank_quantity, blank_quantity, -dissipation_speed * impact_often_measure * agitation_energy - enforcement_weight * radial_distribution * (agitation_energy - 1.0)]
    production_entries = production_entries + [-0.8 * impact_often_measure * unknown_collection[:, k] for k in range(5, 10)]
    production_entries = production_entries + [-0.55 * impact_often_measure * unknown_collection[:, k] for k in range(10, 13)]
    return jnp.stack(production_entries, axis=1)

def section_rate(unknown_collection, grid, rows):
    flux_x, flux_y = fluxes(unknown_collection)
    coeffs = (0.75, -0.15, 1.0 / 60.0)
    along = jnp.zeros_like(flux_x)
    for k in range(3):
        along = along + coeffs[k] * (jnp.roll(flux_x, -(k + 1), axis=2) - jnp.roll(flux_x, k + 1, axis=2))
    lowered = flux_y.astype(jnp.bfloat16)
    across = jnp.dot(grid, lowered.reshape(lowered.shape[0], -1), preferred_element_type=jnp.float32).reshape(unknown_collection.shape)
    return -(along + across) + source(unknown_collection, rows, CROSS_NODES)

def reference(mass_per_volume, motion_speed, agitation_energy, shear_deviatoric, thermal_current_array):
    unknown_collection = jnp.concatenate([mass_per_volume[:, None], motion_speed, agitation_energy[:, None], shear_deviatoric, thermal_current_array], axis=1)
    grid = derivative_rows(0, CROSS_NODES, CROSS_NODES)
    rows = jnp.arange(CROSS_NODES, dtype=jnp.int32)
    first_rate = section_rate(unknown_collection, grid, rows)
    middle = unknown_collection + time_step * first_rate
    second_rate = section_rate(middle, grid, rows)
    return 0.5 * (first_rate + second_rate)
```

```python
import math

import jax
import jax.numpy as jnp
from jax import lax
from jax.experimental import pallas as pl
from jax.experimental.pallas import tpu as pltpu
from jax.sharding import PartitionSpec as P

CROSS_NODES = 1024
LAST = CROSS_NODES - 1
HALF = math.pi / (2.0 * LAST)
MESH = pl.DeviceIdType.MESH

time_step = 0.05
enforcement_weight = 4.0
plate_speed = 0.5
dissipation_speed = 0.25
coeffs = (0.75, -0.15, 1.0 / 60.0)

FIELDS = 13
ROWS = 64
COLS = 128
TILE = 16
PARTS = 4
LAG = 2

SPREAD = [(160.0, 1.25)] + [(40.0, 0.0)] * 3 + [(160.0, 1.25)] + [(50.0, 0.0)] * 8


def encode(value, field):
    rate, centre = SPREAD[field]
    return jnp.exp2(rate * (value - centre)).astype(jnp.bfloat16)


def decode(code, field):
    rate, centre = SPREAD[field]
    return jnp.log(code.astype(jnp.float32)) * (1.0 / (rate * math.log(2.0))) + centre


def flux(u, d):
    temp = u[4]
    speed = u[1:4]
    s = [[u[5], u[6], u[8]], [u[6], u[7], u[9]], [u[8], u[9], -(u[5] + u[7])]]
    q = u[10:13]
    carry = speed[d]
    out = [u[0] * carry]
    for i in range(3):
        term = speed[i] * carry + s[i][d]
        out.append(term + temp if i == d else term)
    out.append(carry * temp + (2.0 / 3.0) * q[d])
    for i, j in ((0, 0), (0, 1), (1, 1), (0, 2), (1, 2)):
        term = carry * s[i][j]
        if i == d and j == d:
            term = term + 0.8 * q[d]
        elif j == d:
            term = term + 0.4 * q[i]
        elif i == d:
            term = term + 0.4 * q[j]
        if i == j:
            term = term - (4.0 / 15.0) * q[d]
        out.append(term)
    for i in range(3):
        term = carry * q[i] + temp * s[i][d]
        out.append(term + 2.5 * temp * temp if i == d else term)
    return out


def source(u, wall):
    rate = u[0] * jnp.sqrt(u[4] * u[4] + 0.25)
    near = jnp.abs(wall)
    out = [None, -enforcement_weight * near * (u[1] - plate_speed * wall), None, None]
    out.append(-dissipation_speed * rate * u[4] - enforcement_weight * near * (u[4] - 1.0))
    out += [-0.8 * rate * u[k] for k in range(5, 10)]
    out += [-0.55 * rate * u[k] for k in range(10, 13)]
    return out


def stencil(f):
    total = None
    for k in range(3):
        term = coeffs[k] * (pltpu.roll(f, COLS - k - 1, 1) - pltpu.roll(f, k + 1, 1))
        total = term if total is None else total + term
    return total


def edges(f, lane):
    out = jnp.zeros_like(f[0])
    for m in range(FIELDS):
        a = pltpu.roll(f[m], 3 * m, 1) if m else f[m]
        out = jnp.where((lane >= 3 * m) & (lane < 3 * m + 3), a, out)
        b = pltpu.roll(f[m], 43 + 3 * m, 1)
        out = jnp.where((lane >= 40 + 3 * m) & (lane < 43 + 3 * m), b, out)
    return out


def mend(diff, lane):
    low = lane < 40
    place = jnp.where(low, lane, lane - 40) % 3
    a1, a2, a3 = coeffs
    right = a3 * diff
    right += jnp.where(place >= 1, a2, 0.0) * pltpu.roll(diff, 1, 1)
    right += jnp.where(place >= 2, a1, 0.0) * pltpu.roll(diff, 2, 1)
    left = a3 * diff
    left += jnp.where(place <= 1, a2, 0.0) * pltpu.roll(diff, COLS - 1, 1)
    left += jnp.where(place == 0, a1, 0.0) * pltpu.roll(diff, COLS - 2, 1)
    return jnp.where(low, right, -left)


def spread(packed, m, lane):
    a = jnp.where(lane >= 125, pltpu.roll(packed, 125 - 3 * m, 1), 0.0)
    return a + jnp.where(lane < 3, pltpu.roll(packed, 88 - 3 * m, 1), 0.0)


def sine(x):
    z = x * x
    poly = 1.0 / 6227020800.0
    for c in (-1.0 / 39916800.0, 1.0 / 362880.0, -1.0 / 5040.0, 1.0 / 120.0, -1.0 / 6.0):
        poly = poly * z + c
    return x + x * z * poly


def grid_block(i, j):
    summed = i + j
    summed = jnp.minimum(summed, 2 * LAST - summed).astype(jnp.float32)
    differ = (i - j).astype(jnp.float32)
    same = i == j
    denom = -2.0 * sine(HALF * summed) * sine(HALF * differ)
    safe = jnp.where(same, 1.0, denom)

    def edge(index):
        return (index == 0) | (index == LAST)

    ratio = jnp.where(edge(i), 2.0, 1.0) * jnp.where(edge(j), 0.5, 1.0)
    ratio = jnp.where((i + j) % 2 == 0, ratio, -ratio)
    wave = sine(HALF * jnp.minimum(2 * i, 2 * (LAST - i)).astype(jnp.float32))
    off = (math.pi / LAST) * wave * ratio / safe
    tall = jnp.where(edge(i), 1.0, wave)
    diagonal = -HALF * sine(HALF * (LAST - 2 * i).astype(jnp.float32)) / tall
    return jnp.where(same, jnp.where(edge(i), 0.0, diagonal), off).astype(jnp.bfloat16)


def kernel(
    rho_ref,
    speed_ref,
    temp_ref,
    shear_ref,
    heat_ref,
    own_ref,
    par_ref,
    U,
    R,
    F1,
    F2,
    enc,
    encr,
    acc,
    ps1,
    pr1,
    ps2,
    pr2,
    D,
    G,
    Go,
    GT,
    GTo,
    GT2,
    H,
    H2,
    TT,
    zs,
    z_s,
    z_r,
    a_s,
    a_r,
    h_s,
    h_r,
    p1_s,
    p1_r,
    f2_s,
    f2_r,
    g_s,
    g_r,
    p2_s,
    p2_r,
    o_s,
    o_r,
):
    gx = lax.axis_index("gx")
    gy = lax.axis_index("gy")
    gxn = lax.axis_size("gx")
    x = gy // 4
    s = (gy // 2) % 2
    c = gy % 2

    def at(dgx, xx, ss, cc):
        return ((gx + dgx + gxn) % gxn, xx * 4 + ss * 2 + cc)

    partner = at(0, x, 1 - s, c)
    sibling = at(0, x, s, 1 - c)
    peers = [at(0, (x + k) % 4, s, c) for k in (1, 2, 3)]
    left_to = at(s - 1, x, 1 - s, c)
    right_to = at(s, x, 1 - s, c)
    beside = at(1 - 2 * s, x, s, c)

    barrier = pltpu.get_barrier_semaphore()
    greet = [partner, sibling, *peers, at(2 * s - 1, x, 1 - s, c), at(1, x, s, c), at(-1, x, s, c)]
    for who in greet:
        pl.semaphore_signal(barrier, inc=1, device_id=who, device_id_type=MESH)

    mine = pl.multiple_of(s * COLS, COLS)
    other = pl.multiple_of((1 - s) * COLS, COLS)
    base = pl.multiple_of(s * ROWS, ROWS)
    pbase = pl.multiple_of((1 - s) * ROWS, ROWS)
    lane = lax.broadcasted_iota(jnp.int32, (TILE, COLS), 1)

    def remote(src, dst, ssem, rsem, who):
        return pltpu.make_async_remote_copy(
            src_ref=src, dst_ref=dst, send_sem=ssem, recv_sem=rsem, device_id=who, device_id_type=MESH
        )

    def inputs(r, col):
        rows, cols = pl.ds(r, TILE), pl.ds(col, COLS)
        u = [rho_ref[rows, cols]]
        u += [speed_ref[k, rows, cols] for k in range(3)]
        u.append(temp_ref[rows, cols])
        u += [shear_ref[k, rows, cols] for k in range(5)]
        u += [heat_ref[k, rows, cols] for k in range(3)]
        return u

    def wall_of(r):
        k = r + lax.broadcasted_iota(jnp.int32, (TILE, COLS), 0)
        row = x * 256 + (r // ROWS) * 128 + c * ROWS + (k - (r // ROWS) * ROWS)
        return jnp.where(row == 0, 1.0, jnp.where(row == LAST, -1.0, 0.0))

    @pl.loop(0, ROWS // TILE)
    def _(t):
        r = pl.multiple_of(t * TILE, TILE)
        u = inputs(r, other)
        for m in range(FIELDS):
            enc[m, pl.ds(r, TILE), :] = encode(u[m], m)
        Go[pl.ds(base + r, TILE), :] = edges(flux(u, 0), lane)
        G[pl.ds(pbase + r, TILE), :] = jnp.zeros((TILE, COLS), jnp.float32)
        Go[pl.ds(pbase + r, TILE), :] = jnp.zeros((TILE, COLS), jnp.float32)

    def first(r, u, side, k):
        rows = pl.ds(r, TILE)
        fy = flux(u, 1)
        for m in range(FIELDS):
            U[m, rows, :] = u[m]
            F1[m, side, x, pl.ds(k, TILE), :] = fy[m].astype(jnp.bfloat16)
        fx = flux(u, 0)
        G[rows, :] = edges(fx, lane)
        src = source(u, wall_of(r))
        for m in range(FIELDS):
            along = stencil(fx[m])
            R[m, rows, :] = -along if src[m] is None else src[m] - along

    @pl.loop(0, ROWS // TILE)
    def _(t):
        r = pl.multiple_of(t * TILE, TILE)
        first(pl.multiple_of(base + r, TILE), inputs(r, mine), s, r)

    GT[...] = G[...].T
    GTo[...] = Go[...].T
    H[s, s] = GTo[pl.ds(pl.multiple_of(40 * s, 8), 40), :]

    pl.semaphore_wait(barrier, len(greet))

    low, high = pl.ds(0, 40), pl.ds(40, 40)
    halos = [
        remote(GT.at[low], H.at[0, s], h_s.at[0], h_r.at[0], left_to),
        remote(GT.at[high], H.at[1, s], h_s.at[1], h_r.at[1], right_to),
        remote(
            GTo.at[pl.ds(pl.multiple_of(40 * (1 - s), 8), 40)],
            H.at[1 - s, s],
            h_s.at[2],
            h_r.at[2],
            beside,
        ),
    ]
    for copy in halos:
        copy.start()

    step = ROWS // PARTS

    def swap(t):
        rows = pl.ds(pl.multiple_of(t * step, step), step)
        return remote(enc.at[:, rows], encr.at[:, rows], z_s.at[t], z_r.at[t], partner)

    for t in range(PARTS):
        swap(t).start()

    def gather_own(k):
        block = F1.at[:, s, x]
        return remote(block, block, a_s.at[PARTS, k], a_r.at[PARTS, k], peers[k])

    def gather_part(t, k):
        block = F1.at[:, 1 - s, x, pl.ds(pl.multiple_of(t * step, step), step)]
        return remote(block, block, a_s.at[t, k], a_r.at[t, k], peers[k])

    for k in range(3):
        gather_own(k).start()

    @pl.loop(0, 256 // TILE)
    def _(t):
        p = pl.multiple_of(t * TILE, TILE)
        row = p + lax.broadcasted_iota(jnp.int32, (TILE, 512), 0)
        rr = row % 128
        core = jnp.where(row < 128, c, 1 - c)
        i = x * 256 + (rr // ROWS) * 128 + core * ROWS + rr % ROWS
        col = lax.broadcasted_iota(jnp.int32, (TILE, 512), 1)
        j = ((col % 256) // ROWS) * 256 + (col // 256) * 128 + c * ROWS + col % ROWS
        D[pl.ds(p, TILE), :] = grid_block(i, j)

    for k in range(3):
        gather_own(k).wait_recv()

    def product(side, m):
        columns = pl.ds(pl.multiple_of(side * 256, 256), 256)
        block = F1[m, side].reshape(256, COLS)
        return jnp.dot(D[:, columns], block, preferred_element_type=jnp.float32)

    @pl.loop(0, FIELDS)
    def _(m):
        acc[m] = product(s, m)

    @pl.loop(0, PARTS)
    def _(t):
        swap(t).wait_recv()

        @pl.loop(0, step // TILE)
        def _(v):
            k = pl.multiple_of(t * step + v * TILE, TILE)
            u = [decode(encr[m, pl.ds(k, TILE), :], m) for m in range(FIELDS)]
            first(pl.multiple_of(pbase + k, TILE), u, 1 - s, k)

        for k in range(3):
            gather_part(t, k).start()

    @pl.loop(0, PARTS)
    def _(t):
        for k in range(3):
            gather_part(t, k).wait_recv()

    def share1(m):
        return remote(ps1.at[m], pr1.at[m], p1_s.at[m], p1_r.at[m], sibling)

    @pl.loop(0, FIELDS)
    def _(m):
        total = acc[m] + product(1 - s, m)
        ps1[m] = total[128:]
        acc[m, pl.ds(0, 128)] = total[:128]
        share1(m).start()

    def packed(rows, right, left):
        TT[pl.ds(0, 40), :] = right
        TT[pl.ds(40, 40), :] = left
        TT[pl.ds(80, 48), :] = jnp.zeros((48, COLS), jnp.float32)
        TT[...] = TT[...].T

    for copy in halos:
        copy.wait_recv()
    packed(None, H[0, 0] + H[0, 1], H[1, 0] + H[1, 1])

    @pl.loop(0, FIELDS)
    def _(m):
        share1(m).wait_recv()

    @pl.loop(0, 128 // TILE)
    def _(t):
        r = pl.multiple_of(t * TILE, TILE)
        rows = pl.ds(r, TILE)
        edge = mend(TT[rows, :] - G[rows, :], lane)
        u, rate = [], []
        for m in range(FIELDS):
            one = R[m, rows, :] - spread(edge, m, lane) - (acc[m, rows, :] + pr1[m, rows, :])
            rate.append(one)
            u.append(U[m, rows, :] + time_step * one)
        fy = flux(u, 1)
        side = r // ROWS
        k = pl.multiple_of(r - side * ROWS, TILE)
        for m in range(FIELDS):
            F2[m, side, x, pl.ds(k, TILE), :] = fy[m].astype(jnp.bfloat16)
        fx = flux(u, 0)
        G[rows, :] = edges(fx, lane)
        src = source(u, wall_of(r))
        for m in range(FIELDS):
            two = rate[m] - stencil(fx[m])
            R[m, rows, :] = 0.5 * (two if src[m] is None else two + src[m])

    def gather2(m, k):
        block = F2.at[m, :, x]
        return remote(block, block, f2_s.at[m, k], f2_r.at[m, k], peers[k])

    GT2[...] = G[...].T
    halos2 = [
        remote(GT2.at[low], H2.at[0], g_s.at[0], g_r.at[0], left_to),
        remote(GT2.at[high], H2.at[1], g_s.at[1], g_r.at[1], right_to),
    ]
    for copy in halos2:
        copy.start()

    @pl.loop(0, FIELDS)
    def _(m):
        for k in range(3):
            gather2(m, k).start()

    def share2(m):
        return remote(ps2.at[m], pr2.at[m], p2_s.at[m], p2_r.at[m], sibling)

    def give(m):
        return remote(zs.at[m], par_ref.at[m], o_s.at[m], o_r.at[m], partner)

    def front(m):
        for k in range(3):
            gather2(m, k).wait_recv()
        total = jnp.dot(D[...], F2[m].reshape(512, COLS), preferred_element_type=jnp.float32)
        ps2[m] = total[128:]
        acc[m, pl.ds(0, 128)] = total[:128]
        share2(m).start()

    def back(m):
        share2(m).wait_recv()

        def value(first_row):
            rows = pl.ds(first_row, ROWS)
            return R[m, rows, :] - 0.5 * (acc[m, rows, :] + pr2[m, rows, :])

        zs[m] = value(pbase).astype(jnp.bfloat16)
        give(m).start()
        own_ref[m] = value(base)

    @pl.loop(0, LAG)
    def _(m):
        front(m)

    for copy in halos2:
        copy.wait_recv()
    packed(None, H2[0], H2[1])

    @pl.loop(0, 128 // TILE)
    def _(t):
        rows = pl.ds(pl.multiple_of(t * TILE, TILE), TILE)
        edge = 0.5 * mend(TT[rows, :] - G[rows, :], lane)
        for m in range(FIELDS):
            R[m, rows, :] = R[m, rows, :] - spread(edge, m, lane)

    @pl.loop(LAG, FIELDS)
    def _(m):
        front(m)
        back(m - LAG)

    @pl.loop(FIELDS - LAG, FIELDS)
    def _(m):
        back(m)

    for copy in halos + halos2:
        copy.wait_send()
    for k in range(3):
        gather_own(k).wait_send()

    @pl.loop(0, PARTS)
    def _(t):
        swap(t).wait_send()
        for k in range(3):
            gather_part(t, k).wait_send()

    @pl.loop(0, FIELDS)
    def _(m):
        share1(m).wait_send()
        share2(m).wait_send()
        for k in range(3):
            gather2(m, k).wait_send()
        give(m).wait_send()

    @pl.loop(0, FIELDS)
    def _(m):
        give(m).wait_recv()


def on_device(mass_per_volume, motion_speed, agitation_energy, shear_deviatoric, thermal_current_array):
    def moved(a):
        return jnp.transpose(a, (1, 0, 2))

    full = (FIELDS, 128, COLS)
    gathered = (FIELDS, 2, 4, ROWS, COLS)
    dma = pltpu.SemaphoreType.DMA
    f32, bf16 = jnp.float32, jnp.bfloat16
    own, par = pl.pallas_call(
        kernel,
        out_shape=(
            jax.ShapeDtypeStruct((FIELDS, ROWS, COLS), f32),
            jax.ShapeDtypeStruct((FIELDS, ROWS, COLS), bf16),
        ),
        in_specs=[pl.BlockSpec(memory_space=pltpu.VMEM)] * 5,
        out_specs=(pl.BlockSpec(memory_space=pltpu.VMEM),) * 2,
        scratch_shapes=[
            pltpu.VMEM(full, f32),
            pltpu.VMEM(full, f32),
            pltpu.VMEM(gathered, bf16),
            pltpu.VMEM(gathered, bf16),
            pltpu.VMEM((FIELDS, ROWS, COLS), bf16),
            pltpu.VMEM((FIELDS, ROWS, COLS), bf16),
            pltpu.VMEM((FIELDS, 256, COLS), f32),
            pltpu.VMEM(full, f32),
            pltpu.VMEM(full, f32),
            pltpu.VMEM(full, f32),
            pltpu.VMEM(full, f32),
            pltpu.VMEM((256, 512), bf16),
            pltpu.VMEM((128, COLS), f32),
            pltpu.VMEM((128, COLS), f32),
            pltpu.VMEM((COLS, 128), f32),
            pltpu.VMEM((COLS, 128), f32),
            pltpu.VMEM((COLS, 128), f32),
            pltpu.VMEM((2, 2, 40, 128), f32),
            pltpu.VMEM((2, 40, 128), f32),
            pltpu.VMEM((128, 128), f32),
            pltpu.VMEM((FIELDS, ROWS, COLS), bf16),
            dma((PARTS,)),
            dma((PARTS,)),
            dma((PARTS + 1, 3)),
            dma((PARTS + 1, 3)),
            dma((3,)),
            dma((3,)),
            dma((FIELDS,)),
            dma((FIELDS,)),
            dma((FIELDS, 3)),
            dma((FIELDS, 3)),
            dma((2,)),
            dma((2,)),
            dma((FIELDS,)),
            dma((FIELDS,)),
            dma((FIELDS,)),
            dma((FIELDS,)),
        ],
        compiler_params=pltpu.CompilerParams(
            collective_id=0, has_side_effects=True, vmem_limit_bytes=40 * 1024 * 1024
        ),
        name="sections",
    )(
        mass_per_volume,
        moved(motion_speed),
        agitation_energy,
        moved(shear_deviatoric),
        moved(thermal_current_array),
    )
    par = par.astype(f32)
    lower = (lax.axis_index("gy") // 2) % 2 == 0
    halves = [jnp.where(lower, own, par), jnp.where(lower, par, own)]
    return jnp.transpose(jnp.concatenate(halves, axis=2), (1, 0, 2))


def solution(mesh):
    return jax.shard_map(
        on_device,
        mesh=mesh,
        in_specs=(
            P("gy", "gx"),
            P("gy", None, "gx"),
            P("gy", "gx"),
            P("gy", None, "gx"),
            P("gy", None, "gx"),
        ),
        out_specs=P("gy", None, "gx"),
        check_vma=False,
    )
```

```python
import math

import jax
import jax.numpy as jnp
from jax import lax
from jax.experimental import pallas as pl
from jax.experimental.pallas import tpu as pltpu
from jax.sharding import PartitionSpec as P

CROSS_NODES = 1024
LAST = CROSS_NODES - 1
HALF = math.pi / (2.0 * LAST)
MESH = pl.DeviceIdType.MESH

time_step = 0.05
enforcement_weight = 4.0
plate_speed = 0.5
dissipation_speed = 0.25
coeffs = (0.75, -0.15, 1.0 / 60.0)

FIELDS = 13
ROWS = 64
COLS = 128
TILE = 16
PARTS = 4
LAG = 2

SPREAD = [(160.0, 1.25)] + [(40.0, 0.0)] * 3 + [(160.0, 1.25)] + [(50.0, 0.0)] * 8


def encode(value, field):
    rate, centre = SPREAD[field]
    return jnp.exp2(rate * (value - centre)).astype(jnp.bfloat16)


def decode(code, field):
    rate, centre = SPREAD[field]
    return jnp.log(code.astype(jnp.float32)) * (1.0 / (rate * math.log(2.0))) + centre


def flux(u, d):
    temp = u[4]
    speed = u[1:4]
    s = [[u[5], u[6], u[8]], [u[6], u[7], u[9]], [u[8], u[9], -(u[5] + u[7])]]
    q = u[10:13]
    carry = speed[d]
    out = [u[0] * carry]
    for i in range(3):
        term = speed[i] * carry + s[i][d]
        out.append(term + temp if i == d else term)
    out.append(carry * temp + (2.0 / 3.0) * q[d])
    for i, j in ((0, 0), (0, 1), (1, 1), (0, 2), (1, 2)):
        term = carry * s[i][j]
        if i == d and j == d:
            term = term + 0.8 * q[d]
        elif j == d:
            term = term + 0.4 * q[i]
        elif i == d:
            term = term + 0.4 * q[j]
        if i == j:
            term = term - (4.0 / 15.0) * q[d]
        out.append(term)
    for i in range(3):
        term = carry * q[i] + temp * s[i][d]
        out.append(term + 2.5 * temp * temp if i == d else term)
    return out


def source(u, wall):
    rate = u[0] * jnp.sqrt(u[4] * u[4] + 0.25)
    near = jnp.abs(wall)
    out = [None, -enforcement_weight * near * (u[1] - plate_speed * wall), None, None]
    out.append(-dissipation_speed * rate * u[4] - enforcement_weight * near * (u[4] - 1.0))
    out += [-0.8 * rate * u[k] for k in range(5, 10)]
    out += [-0.55 * rate * u[k] for k in range(10, 13)]
    return out


def stencil(f):
    total = None
    for k in range(3):
        term = coeffs[k] * (pltpu.roll(f, COLS - k - 1, 1) - pltpu.roll(f, k + 1, 1))
        total = term if total is None else total + term
    return total


def edges(f, lane):
    out = jnp.zeros_like(f[0])
    for m in range(FIELDS):
        a = pltpu.roll(f[m], 3 * m, 1) if m else f[m]
        out = jnp.where((lane >= 3 * m) & (lane < 3 * m + 3), a, out)
        b = pltpu.roll(f[m], 43 + 3 * m, 1)
        out = jnp.where((lane >= 40 + 3 * m) & (lane < 43 + 3 * m), b, out)
    return out


def mend(diff, lane):
    low = lane < 40
    place = jnp.where(low, lane, lane - 40) % 3
    a1, a2, a3 = coeffs
    right = a3 * diff
    right += jnp.where(place >= 1, a2, 0.0) * pltpu.roll(diff, 1, 1)
    right += jnp.where(place >= 2, a1, 0.0) * pltpu.roll(diff, 2, 1)
    left = a3 * diff
    left += jnp.where(place <= 1, a2, 0.0) * pltpu.roll(diff, COLS - 1, 1)
    left += jnp.where(place == 0, a1, 0.0) * pltpu.roll(diff, COLS - 2, 1)
    return jnp.where(low, right, -left)


def spread(packed, m, lane):
    a = jnp.where(lane >= 125, pltpu.roll(packed, 125 - 3 * m, 1), 0.0)
    return a + jnp.where(lane < 3, pltpu.roll(packed, 88 - 3 * m, 1), 0.0)


def sine(x):
    z = x * x
    poly = 1.0 / 6227020800.0
    for c in (-1.0 / 39916800.0, 1.0 / 362880.0, -1.0 / 5040.0, 1.0 / 120.0, -1.0 / 6.0):
        poly = poly * z + c
    return x + x * z * poly


def grid_block(i, j):
    summed = i + j
    summed = jnp.minimum(summed, 2 * LAST - summed).astype(jnp.float32)
    differ = (i - j).astype(jnp.float32)
    same = i == j
    denom = -2.0 * sine(HALF * summed) * sine(HALF * differ)
    safe = jnp.where(same, 1.0, denom)

    def edge(index):
        return (index == 0) | (index == LAST)

    ratio = jnp.where(edge(i), 2.0, 1.0) * jnp.where(edge(j), 0.5, 1.0)
    ratio = jnp.where((i + j) % 2 == 0, ratio, -ratio)
    wave = sine(HALF * jnp.minimum(2 * i, 2 * (LAST - i)).astype(jnp.float32))
    off = (math.pi / LAST) * wave * ratio / safe
    tall = jnp.where(edge(i), 1.0, wave)
    diagonal = -HALF * sine(HALF * (LAST - 2 * i).astype(jnp.float32)) / tall
    return jnp.where(same, jnp.where(edge(i), 0.0, diagonal), off).astype(jnp.bfloat16)


def kernel(
    rho_ref,
    speed_ref,
    temp_ref,
    shear_ref,
    heat_ref,
    own_ref,
    par_ref,
    U,
    R,
    F1,
    F2,
    enc,
    encr,
    acc,
    ps1,
    pr1,
    ps2,
    pr2,
    D,
    G,
    GT1,
    GT2,
    H1,
    H2,
    TT,
    X,
    zs,
    in_s,
    z_s,
    z_r,
    a_s,
    a_r,
    h_s,
    h_r,
    p1_s,
    p1_r,
    f2_s,
    f2_r,
    g_s,
    g_r,
    p2_s,
    p2_r,
    o_s,
    o_r,
):
    gx = lax.axis_index("gx")
    gy = lax.axis_index("gy")
    gxn = lax.axis_size("gx")
    x = gy // 4
    s = (gy // 2) % 2
    c = gy % 2

    def at(dgx, xx, ss, cc):
        return ((gx + dgx + gxn) % gxn, xx * 4 + ss * 2 + cc)

    partner = at(0, x, 1 - s, c)
    sibling = at(0, x, s, 1 - c)
    peers = [at(0, (x + k) % 4, s, c) for k in (1, 2, 3)]
    left_to = at(s - 1, x, 1 - s, c)
    right_to = at(s, x, 1 - s, c)

    barrier = pltpu.get_barrier_semaphore()
    greet = [partner, sibling, *peers, at(2 * s - 1, x, 1 - s, c)]
    for who in greet:
        pl.semaphore_signal(barrier, inc=1, device_id=who, device_id_type=MESH)

    mine = pl.multiple_of(s * COLS, COLS)
    other = pl.multiple_of((1 - s) * COLS, COLS)
    base = pl.multiple_of(s * ROWS, ROWS)
    pbase = pl.multiple_of((1 - s) * ROWS, ROWS)
    lane = lax.broadcasted_iota(jnp.int32, (TILE, COLS), 1)

    def remote(src, dst, ssem, rsem, who):
        return pltpu.make_async_remote_copy(
            src_ref=src, dst_ref=dst, send_sem=ssem, recv_sem=rsem, device_id=who, device_id_type=MESH
        )

    def load(half, column):
        cols = pl.ds(column, COLS)
        groups = ((rho_ref, 0, 0), (speed_ref, 1, 3), (temp_ref, 4, 0), (shear_ref, 5, 5), (heat_ref, 10, 3))
        copies = []
        for n, (ref, start, count) in enumerate(groups):
            src = ref.at[:, :, cols] if count else ref.at[:, cols]
            dst = X.at[half, pl.ds(start, count)] if count else X.at[half, start]
            copies.append(pltpu.make_async_copy(src, dst, in_s.at[half, n]))
        return copies

    loads = [load(0, other), load(1, mine)]
    for copy in loads[0] + loads[1]:
        copy.start()

    def inputs(half, r):
        return [X[half, m, pl.ds(r, TILE), :] for m in range(FIELDS)]

    def wall_of(r):
        k = r + lax.broadcasted_iota(jnp.int32, (TILE, COLS), 0)
        row = x * 256 + (r // ROWS) * 128 + c * ROWS + (k - (r // ROWS) * ROWS)
        return jnp.where(row == 0, 1.0, jnp.where(row == LAST, -1.0, 0.0))

    for copy in loads[0]:
        copy.wait()

    @pl.loop(0, ROWS // TILE)
    def _(t):
        r = pl.multiple_of(t * TILE, TILE)
        u = inputs(0, r)
        for m in range(FIELDS):
            enc[m, pl.ds(r, TILE), :] = encode(u[m], m)

    pl.semaphore_wait(barrier, len(greet))

    step = ROWS // PARTS

    def swap(t):
        rows = pl.ds(pl.multiple_of(t * step, step), step)
        return remote(enc.at[:, rows], encr.at[:, rows], z_s.at[t], z_r.at[t], partner)

    for t in range(PARTS):
        swap(t).start()

    def first(r, u, side, k):
        rows = pl.ds(r, TILE)
        fy = flux(u, 1)
        for m in range(FIELDS):
            U[m, rows, :] = u[m]
            F1[m, side, x, pl.ds(k, TILE), :] = fy[m].astype(jnp.bfloat16)
        fx = flux(u, 0)
        G[rows, :] = edges(fx, lane)
        src = source(u, wall_of(r))
        for m in range(FIELDS):
            along = stencil(fx[m])
            R[m, rows, :] = -along if src[m] is None else src[m] - along

    for copy in loads[1]:
        copy.wait()

    @pl.loop(0, ROWS // TILE)
    def _(t):
        r = pl.multiple_of(t * TILE, TILE)
        first(pl.multiple_of(base + r, TILE), inputs(1, r), s, r)

    def gather_own(k):
        block = F1.at[:, s, x]
        return remote(block, block, a_s.at[PARTS, k], a_r.at[PARTS, k], peers[k])

    def gather_part(t, k):
        block = F1.at[:, 1 - s, x, pl.ds(pl.multiple_of(t * step, step), step)]
        return remote(block, block, a_s.at[t, k], a_r.at[t, k], peers[k])

    for k in range(3):
        gather_own(k).start()

    @pl.loop(0, 256 // TILE)
    def _(t):
        p = pl.multiple_of(t * TILE, TILE)
        row = p + lax.broadcasted_iota(jnp.int32, (TILE, 512), 0)
        rr = row % 128
        core = jnp.where(row < 128, c, 1 - c)
        i = x * 256 + (rr // ROWS) * 128 + core * ROWS + rr % ROWS
        col = lax.broadcasted_iota(jnp.int32, (TILE, 512), 1)
        j = ((col % 256) // ROWS) * 256 + (col // 256) * 128 + c * ROWS + col % ROWS
        D[pl.ds(p, TILE), :] = grid_block(i, j)

    for k in range(3):
        gather_own(k).wait_recv()

    def product(side, fields):
        columns = pl.ds(pl.multiple_of(side * 256, 256), 256)
        blocks = [F1[m, side].reshape(256, COLS) for m in fields]
        block = jnp.concatenate(blocks, axis=1) if len(blocks) > 1 else blocks[0]
        total = jnp.dot(D[:, columns], block, preferred_element_type=jnp.float32)
        return [total[:, n * COLS : (n + 1) * COLS] for n in range(len(blocks))]

    def in_pairs(body):
        @pl.loop(0, FIELDS // 2)
        def _(p):
            body((2 * p, 2 * p + 1))

        body((FIELDS - 1,))

    def own_side(fields):
        for m, total in zip(fields, product(s, fields)):
            acc[m] = total

    in_pairs(own_side)

    @pl.loop(0, PARTS)
    def _(t):
        swap(t).wait_recv()

        @pl.loop(0, step // TILE)
        def _(v):
            k = pl.multiple_of(t * step + v * TILE, TILE)
            u = [decode(encr[m, pl.ds(k, TILE), :], m) for m in range(FIELDS)]
            first(pl.multiple_of(pbase + k, TILE), u, 1 - s, k)

        for k in range(3):
            gather_part(t, k).start()

    low, high = pl.ds(0, 40), pl.ds(40, 40)

    def send_edges(GT, H, ssem, rsem):
        GT[...] = G[...].T
        copies = [
            remote(GT.at[low], H.at[0], ssem.at[0], rsem.at[0], left_to),
            remote(GT.at[high], H.at[1], ssem.at[1], rsem.at[1], right_to),
        ]
        for copy in copies:
            copy.start()
        return copies

    halos1 = send_edges(GT1, H1, h_s, h_r)

    @pl.loop(0, PARTS)
    def _(t):
        for k in range(3):
            gather_part(t, k).wait_recv()

    def share1(m):
        return remote(ps1.at[m], pr1.at[m], p1_s.at[m], p1_r.at[m], sibling)

    def other_side(fields):
        for m, total in zip(fields, product(1 - s, fields)):
            ps1[m] = acc[m, pl.ds(128, 128)] + total[128:]
            share1(m).start()
            acc[m, pl.ds(0, 128)] += total[:128]

    in_pairs(other_side)

    def receive_edges(copies, H):
        for copy in copies:
            copy.wait_recv()
        TT[low, :] = H[0]
        TT[high, :] = H[1]
        TT[pl.ds(80, 48), :] = jnp.zeros((48, COLS), jnp.float32)
        TT[...] = TT[...].T

    receive_edges(halos1, H1)

    @pl.loop(0, FIELDS)
    def _(m):
        share1(m).wait_recv()

    @pl.loop(0, 128 // TILE)
    def _(t):
        r = pl.multiple_of(t * TILE, TILE)
        rows = pl.ds(r, TILE)
        edge = mend(TT[rows, :] - G[rows, :], lane)
        u, rate = [], []
        for m in range(FIELDS):
            one = R[m, rows, :] - spread(edge, m, lane) - (acc[m, rows, :] + pr1[m, rows, :])
            rate.append(one)
            u.append(U[m, rows, :] + time_step * one)
        fy = flux(u, 1)
        side = r // ROWS
        k = pl.multiple_of(r - side * ROWS, TILE)
        for m in range(FIELDS):
            F2[m, side, x, pl.ds(k, TILE), :] = fy[m].astype(jnp.bfloat16)
        fx = flux(u, 0)
        G[rows, :] = edges(fx, lane)
        src = source(u, wall_of(r))
        for m in range(FIELDS):
            two = rate[m] - stencil(fx[m])
            R[m, rows, :] = 0.5 * (two if src[m] is None else two + src[m])

    def gather2(m, k):
        block = F2.at[m, :, x]
        return remote(block, block, f2_s.at[m, k], f2_r.at[m, k], peers[k])

    @pl.loop(0, FIELDS)
    def _(m):
        for k in range(3):
            gather2(m, k).start()

    halos2 = send_edges(GT2, H2, g_s, g_r)

    def share2(m):
        return remote(ps2.at[m], pr2.at[m], p2_s.at[m], p2_r.at[m], sibling)

    def give(m):
        return remote(zs.at[m], par_ref.at[m], o_s.at[m], o_r.at[m], partner)

    def front(m):
        for k in range(3):
            gather2(m, k).wait_recv()
        total = jnp.dot(D[...], F2[m].reshape(512, COLS), preferred_element_type=jnp.float32)
        ps2[m] = total[128:]
        acc[m, pl.ds(0, 128)] = total[:128]
        share2(m).start()

    def back(m):
        share2(m).wait_recv()

        def value(first_row):
            rows = pl.ds(first_row, ROWS)
            return R[m, rows, :] - 0.5 * (acc[m, rows, :] + pr2[m, rows, :])

        zs[m] = value(pbase).astype(jnp.bfloat16)
        give(m).start()
        own_ref[m] = value(base)

    @pl.loop(0, LAG)
    def _(m):
        front(m)

    receive_edges(halos2, H2)

    @pl.loop(0, 128 // TILE)
    def _(t):
        rows = pl.ds(pl.multiple_of(t * TILE, TILE), TILE)
        edge = 0.5 * mend(TT[rows, :] - G[rows, :], lane)
        for m in range(FIELDS):
            R[m, rows, :] = R[m, rows, :] - spread(edge, m, lane)

    @pl.loop(LAG, FIELDS)
    def _(m):
        front(m)
        back(m - LAG)

    @pl.loop(FIELDS - LAG, FIELDS)
    def _(m):
        back(m)

    for copy in halos1 + halos2:
        copy.wait_send()
    for k in range(3):
        gather_own(k).wait_send()

    @pl.loop(0, PARTS)
    def _(t):
        swap(t).wait_send()
        for k in range(3):
            gather_part(t, k).wait_send()

    @pl.loop(0, FIELDS)
    def _(m):
        share1(m).wait_send()
        share2(m).wait_send()
        for k in range(3):
            gather2(m, k).wait_send()
        give(m).wait_send()

    @pl.loop(0, FIELDS)
    def _(m):
        give(m).wait_recv()


def on_device(mass_per_volume, motion_speed, agitation_energy, shear_deviatoric, thermal_current_array):
    def moved(a):
        return jnp.transpose(a, (1, 0, 2))

    full = (FIELDS, 128, COLS)
    gathered = (FIELDS, 2, 4, ROWS, COLS)
    dma = pltpu.SemaphoreType.DMA
    f32, bf16 = jnp.float32, jnp.bfloat16
    own, par = pl.pallas_call(
        kernel,
        out_shape=(
            jax.ShapeDtypeStruct((FIELDS, ROWS, COLS), f32),
            jax.ShapeDtypeStruct((FIELDS, ROWS, COLS), bf16),
        ),
        in_specs=[pl.BlockSpec(memory_space=pltpu.HBM)] * 5,
        out_specs=(pl.BlockSpec(memory_space=pltpu.VMEM),) * 2,
        scratch_shapes=[
            pltpu.VMEM(full, f32),
            pltpu.VMEM(full, f32),
            pltpu.VMEM(gathered, bf16),
            pltpu.VMEM(gathered, bf16),
            pltpu.VMEM((FIELDS, ROWS, COLS), bf16),
            pltpu.VMEM((FIELDS, ROWS, COLS), bf16),
            pltpu.VMEM((FIELDS, 256, COLS), f32),
            pltpu.VMEM(full, f32),
            pltpu.VMEM(full, f32),
            pltpu.VMEM(full, f32),
            pltpu.VMEM(full, f32),
            pltpu.VMEM((256, 512), bf16),
            pltpu.VMEM((128, COLS), f32),
            pltpu.VMEM((COLS, 128), f32),
            pltpu.VMEM((COLS, 128), f32),
            pltpu.VMEM((2, 40, 128), f32),
            pltpu.VMEM((2, 40, 128), f32),
            pltpu.VMEM((128, 128), f32),
            pltpu.VMEM((2, FIELDS, ROWS, COLS), f32),
            pltpu.VMEM((FIELDS, ROWS, COLS), bf16),
            dma((2, 5)),
            dma((PARTS,)),
            dma((PARTS,)),
            dma((PARTS + 1, 3)),
            dma((PARTS + 1, 3)),
            dma((2,)),
            dma((2,)),
            dma((FIELDS,)),
            dma((FIELDS,)),
            dma((FIELDS, 3)),
            dma((FIELDS, 3)),
            dma((2,)),
            dma((2,)),
            dma((FIELDS,)),
            dma((FIELDS,)),
            dma((FIELDS,)),
            dma((FIELDS,)),
        ],
        compiler_params=pltpu.CompilerParams(
            collective_id=0, has_side_effects=True, vmem_limit_bytes=66_500_000
        ),
        name="sections",
    )(
        mass_per_volume,
        moved(motion_speed),
        agitation_energy,
        moved(shear_deviatoric),
        moved(thermal_current_array),
    )
    par = par.astype(f32)
    lower = (lax.axis_index("gy") // 2) % 2 == 0
    halves = [jnp.where(lower, own, par), jnp.where(lower, par, own)]
    return jnp.transpose(jnp.concatenate(halves, axis=2), (1, 0, 2))


def solution(mesh):
    return jax.shard_map(
        on_device,
        mesh=mesh,
        in_specs=(
            P("gy", "gx"),
            P("gy", None, "gx"),
            P("gy", "gx"),
            P("gy", None, "gx"),
            P("gy", None, "gx"),
        ),
        out_specs=P("gy", None, "gx"),
        check_vma=False,
    )
```

```python
import math

import jax
import jax.numpy as jnp
from jax import lax
from jax.experimental import pallas as pl
from jax.experimental.pallas import tpu as pltpu
from jax.sharding import PartitionSpec as P

CROSS_NODES = 1024
LAST = CROSS_NODES - 1
HALF = math.pi / (2.0 * LAST)
MESH = pl.DeviceIdType.MESH

time_step = 0.05
enforcement_weight = 4.0
plate_speed = 0.5
dissipation_speed = 0.25
coeffs = (0.75, -0.15, 1.0 / 60.0)

FIELDS = 13
ROWS = 64
COLS = 128
TILE = 16
PARTS = ROWS // TILE
LEAD = 3

SPREAD = [(160.0, 1.25)] + [(40.0, 0.0)] * 3 + [(160.0, 1.25)] + [(50.0, 0.0)] * 8


def encode(value, field):
    rate, centre = SPREAD[field]
    return jnp.exp2(rate * (value - centre)).astype(jnp.bfloat16)


def decode(code, field):
    rate, centre = SPREAD[field]
    return jnp.log(code.astype(jnp.float32)) * (1.0 / (rate * math.log(2.0))) + centre


def flux(u, d):
    temp = u[4]
    speed = u[1:4]
    s = [[u[5], u[6], u[8]], [u[6], u[7], u[9]], [u[8], u[9], -(u[5] + u[7])]]
    q = u[10:13]
    carry = speed[d]
    out = [u[0] * carry]
    for i in range(3):
        term = speed[i] * carry + s[i][d]
        out.append(term + temp if i == d else term)
    out.append(carry * temp + (2.0 / 3.0) * q[d])
    for i, j in ((0, 0), (0, 1), (1, 1), (0, 2), (1, 2)):
        term = carry * s[i][j]
        if i == d and j == d:
            term = term + 0.8 * q[d]
        elif j == d:
            term = term + 0.4 * q[i]
        elif i == d:
            term = term + 0.4 * q[j]
        if i == j:
            term = term - (4.0 / 15.0) * q[d]
        out.append(term)
    for i in range(3):
        term = carry * q[i] + temp * s[i][d]
        out.append(term + 2.5 * temp * temp if i == d else term)
    return out


def source(u, wall):
    rate = u[0] * jnp.sqrt(u[4] * u[4] + 0.25)
    near = jnp.abs(wall)
    out = [None, -enforcement_weight * near * (u[1] - plate_speed * wall), None, None]
    out.append(-dissipation_speed * rate * u[4] - enforcement_weight * near * (u[4] - 1.0))
    out += [-0.8 * rate * u[k] for k in range(5, 10)]
    out += [-0.55 * rate * u[k] for k in range(10, 13)]
    return out


def stencil(f):
    total = None
    for k in range(3):
        term = coeffs[k] * (pltpu.roll(f, COLS - k - 1, 1) - pltpu.roll(f, k + 1, 1))
        total = term if total is None else total + term
    return total


def edges(f, lane):
    out = jnp.zeros_like(f[0])
    for m in range(FIELDS):
        a = pltpu.roll(f[m], 3 * m, 1) if m else f[m]
        out = jnp.where((lane >= 3 * m) & (lane < 3 * m + 3), a, out)
        b = pltpu.roll(f[m], 43 + 3 * m, 1)
        out = jnp.where((lane >= 40 + 3 * m) & (lane < 43 + 3 * m), b, out)
    return out


def mend(diff, lane):
    low = lane < 40
    place = jnp.where(low, lane, lane - 40) % 3
    a1, a2, a3 = coeffs
    right = a3 * diff
    right += jnp.where(place >= 1, a2, 0.0) * pltpu.roll(diff, 1, 1)
    right += jnp.where(place >= 2, a1, 0.0) * pltpu.roll(diff, 2, 1)
    left = a3 * diff
    left += jnp.where(place <= 1, a2, 0.0) * pltpu.roll(diff, COLS - 1, 1)
    left += jnp.where(place == 0, a1, 0.0) * pltpu.roll(diff, COLS - 2, 1)
    return jnp.where(low, right, -left)


def spread(packed, m, lane):
    a = jnp.where(lane >= 125, pltpu.roll(packed, 125 - 3 * m, 1), 0.0)
    return a + jnp.where(lane < 3, pltpu.roll(packed, 88 - 3 * m, 1), 0.0)


def sine(x):
    z = x * x
    poly = 1.0 / 6227020800.0
    for c in (-1.0 / 39916800.0, 1.0 / 362880.0, -1.0 / 5040.0, 1.0 / 120.0, -1.0 / 6.0):
        poly = poly * z + c
    return x + x * z * poly


def grid_block(i, j):
    summed = i + j
    summed = jnp.minimum(summed, 2 * LAST - summed).astype(jnp.float32)
    differ = (i - j).astype(jnp.float32)
    same = i == j
    denom = -2.0 * sine(HALF * summed) * sine(HALF * differ)
    safe = jnp.where(same, 1.0, denom)

    def edge(index):
        return (index == 0) | (index == LAST)

    ratio = jnp.where(edge(i), 2.0, 1.0) * jnp.where(edge(j), 0.5, 1.0)
    ratio = jnp.where((i + j) % 2 == 0, ratio, -ratio)
    wave = sine(HALF * jnp.minimum(2 * i, 2 * (LAST - i)).astype(jnp.float32))
    off = (math.pi / LAST) * wave * ratio / safe
    tall = jnp.where(edge(i), 1.0, wave)
    diagonal = -HALF * sine(HALF * (LAST - 2 * i).astype(jnp.float32)) / tall
    return jnp.where(same, jnp.where(edge(i), 0.0, diagonal), off).astype(jnp.bfloat16)


def kernel(
    rho_ref,
    speed_ref,
    temp_ref,
    shear_ref,
    heat_ref,
    OUT,
    par,
    U,
    FX,
    R,
    F1,
    F2,
    enc,
    encr,
    acc,
    ps1,
    pr1,
    ps2,
    pr2,
    D,
    G,
    GT1,
    GT2,
    H1,
    H2,
    TT,
    X,
    zs,
    in_s,
    z_s,
    z_r,
    a_s,
    a_r,
    h_s,
    h_r,
    p1_s,
    p1_r,
    f2_s,
    f2_r,
    g_s,
    g_r,
    p2_s,
    p2_r,
    o_s,
    o_r,
):
    gx = lax.axis_index("gx")
    gy = lax.axis_index("gy")
    gxn = lax.axis_size("gx")
    x = gy // 4
    s = (gy // 2) % 2
    c = gy % 2

    def at(dgx, xx, ss, cc):
        return ((gx + dgx + gxn) % gxn, xx * 4 + ss * 2 + cc)

    partner = at(0, x, 1 - s, c)
    sibling = at(0, x, s, 1 - c)
    peers = [at(0, (x + k) % 4, s, c) for k in (1, 2, 3)]
    left_to = at(s - 1, x, 1 - s, c)
    right_to = at(s, x, 1 - s, c)

    barrier = pltpu.get_barrier_semaphore()
    greet = [partner, sibling, *peers, at(2 * s - 1, x, 1 - s, c)]
    for who in greet:
        pl.semaphore_signal(barrier, inc=1, device_id=who, device_id_type=MESH)

    mine = pl.multiple_of(s * COLS, COLS)
    other = pl.multiple_of((1 - s) * COLS, COLS)
    base = pl.multiple_of(s * ROWS, ROWS)
    pbase = pl.multiple_of((1 - s) * ROWS, ROWS)
    lane = lax.broadcasted_iota(jnp.int32, (TILE, COLS), 1)

    def remote(src, dst, ssem, rsem, who):
        return pltpu.make_async_remote_copy(
            src_ref=src, dst_ref=dst, send_sem=ssem, recv_sem=rsem, device_id=who, device_id_type=MESH
        )

    def load(half, column):
        cols = pl.ds(column, COLS)
        groups = ((rho_ref, 0, 0), (speed_ref, 1, 3), (temp_ref, 4, 0), (shear_ref, 5, 5), (heat_ref, 10, 3))
        copies = []
        for n, (ref, start, count) in enumerate(groups):
            src = ref.at[:, :, cols] if count else ref.at[:, cols]
            dst = X.at[half, pl.ds(start, count)] if count else X.at[half, start]
            copies.append(pltpu.make_async_copy(src, dst, in_s.at[half, n]))
        return copies

    loads = [load(0, other), load(1, mine)]
    for copy in loads[0] + loads[1]:
        copy.start()

    def inputs(half, r):
        return [X[half, m, pl.ds(r, TILE), :] for m in range(FIELDS)]

    def wall_of(r):
        k = r + lax.broadcasted_iota(jnp.int32, (TILE, COLS), 0)
        row = x * 256 + (r // ROWS) * 128 + c * ROWS + (k - (r // ROWS) * ROWS)
        return jnp.where(row == 0, 1.0, jnp.where(row == LAST, -1.0, 0.0))

    for copy in loads[0]:
        copy.wait()

    @pl.loop(0, ROWS // TILE)
    def _(t):
        r = pl.multiple_of(t * TILE, TILE)
        u = inputs(0, r)
        for m in range(FIELDS):
            enc[m, pl.ds(r, TILE), :] = encode(u[m], m)

    pl.semaphore_wait(barrier, len(greet))

    def swap(t):
        rows = pl.ds(pl.multiple_of(t * TILE, TILE), TILE)
        return remote(enc.at[:, rows], encr.at[:, rows], z_s.at[t], z_r.at[t], partner)

    for t in range(PARTS):
        swap(t).start()

    def across_flux(F, u, side, k):
        fy = flux(u, 1)
        for m in range(FIELDS):
            F[m, side, x, pl.ds(k, TILE), :] = fy[m].astype(jnp.bfloat16)

    def first(r, u):
        rows = pl.ds(r, TILE)
        for m in range(FIELDS):
            U[m, rows, :] = u[m]
        fx = flux(u, 0)
        G[rows, :] = edges(fx, lane)
        src = source(u, wall_of(r))
        for m in range(FIELDS):
            along = stencil(fx[m])
            R[m, rows, :] = -along if src[m] is None else src[m] - along

    for copy in loads[1]:
        copy.wait()

    @pl.loop(0, ROWS // TILE)
    def _(t):
        r = pl.multiple_of(t * TILE, TILE)
        u = inputs(1, r)
        across_flux(F1, u, s, r)
        first(pl.multiple_of(base + r, TILE), u)

    def gather_own(k):
        block = F1.at[:, s, x]
        return remote(block, block, a_s.at[PARTS, k], a_r.at[PARTS, k], peers[k])

    def gather_part(t, k):
        block = F1.at[:, 1 - s, x, pl.ds(pl.multiple_of(t * TILE, TILE), TILE)]
        return remote(block, block, a_s.at[t, k], a_r.at[t, k], peers[k])

    for k in range(3):
        gather_own(k).start()

    @pl.loop(0, 256 // TILE)
    def _(t):
        p = pl.multiple_of(t * TILE, TILE)
        row = p + lax.broadcasted_iota(jnp.int32, (TILE, 512), 0)
        rr = row % 128
        core = jnp.where(row < 128, c, 1 - c)
        i = x * 256 + (rr // ROWS) * 128 + core * ROWS + rr % ROWS
        col = lax.broadcasted_iota(jnp.int32, (TILE, 512), 1)
        j = ((col % 256) // ROWS) * 256 + (col // 256) * 128 + c * ROWS + col % ROWS
        D[pl.ds(p, TILE), :] = grid_block(i, j)

    for k in range(3):
        gather_own(k).wait_recv()

    def product(side, fields):
        columns = pl.ds(pl.multiple_of(side * 256, 256), 256)
        blocks = [F1[m, side].reshape(256, COLS) for m in fields]
        block = jnp.concatenate(blocks, axis=1) if len(blocks) > 1 else blocks[0]
        total = jnp.dot(D[:, columns], block, preferred_element_type=jnp.float32)
        return [total[:, n * COLS : (n + 1) * COLS] for n in range(len(blocks))]

    def in_pairs(body):
        @pl.loop(0, FIELDS // 2)
        def _(p):
            body((2 * p, 2 * p + 1))

        body((FIELDS - 1,))

    def own_side(fields):
        for m, total in zip(fields, product(s, fields)):
            acc[m] = total

    in_pairs(own_side)

    @pl.loop(0, PARTS)
    def _(t):
        swap(t).wait_recv()
        r = pl.multiple_of(t * TILE, TILE)
        u = [decode(encr[m, pl.ds(r, TILE), :], m) for m in range(FIELDS)]
        across_flux(F1, u, 1 - s, r)
        for k in range(3):
            gather_part(t, k).start()
        first(pl.multiple_of(pbase + r, TILE), u)

    low, high = pl.ds(0, 40), pl.ds(40, 40)

    def send_edges(GT, H, ssem, rsem):
        GT[...] = G[...].T
        copies = [
            remote(GT.at[low], H.at[0], ssem.at[0], rsem.at[0], left_to),
            remote(GT.at[high], H.at[1], ssem.at[1], rsem.at[1], right_to),
        ]
        for copy in copies:
            copy.start()
        return copies

    halos1 = send_edges(GT1, H1, h_s, h_r)

    @pl.loop(0, PARTS)
    def _(t):
        for k in range(3):
            gather_part(t, k).wait_recv()

    def share1(m):
        return remote(ps1.at[m], pr1.at[m], p1_s.at[m], p1_r.at[m], sibling)

    def other_side(fields):
        for m, total in zip(fields, product(1 - s, fields)):
            ps1[m] = acc[m, pl.ds(128, 128)] + total[128:]
            share1(m).start()
            acc[m, pl.ds(0, 128)] += total[:128]

    in_pairs(other_side)

    def receive_edges(copies, H):
        for copy in copies:
            copy.wait_recv()
        TT[low, :] = H[0]
        TT[high, :] = H[1]
        TT[pl.ds(80, 48), :] = jnp.zeros((48, COLS), jnp.float32)
        TT[...] = TT[...].T

    receive_edges(halos1, H1)

    @pl.loop(0, FIELDS)
    def _(m):
        share1(m).wait_recv()

    @pl.loop(0, 128 // TILE)
    def _(t):
        r = pl.multiple_of(t * TILE, TILE)
        rows = pl.ds(r, TILE)
        edge = mend(TT[rows, :] - G[rows, :], lane)
        u = []
        for m in range(FIELDS):
            one = R[m, rows, :] - spread(edge, m, lane) - (acc[m, rows, :] + pr1[m, rows, :])
            R[m, rows, :] = one
            u.append(U[m, rows, :] + time_step * one)
            U[m, rows, :] = u[m]
        side = r // ROWS
        across_flux(F2, u, side, pl.multiple_of(r - side * ROWS, TILE))
        fx = flux(u, 0)
        for m in range(FIELDS):
            FX[m, rows, :] = fx[m]
        G[rows, :] = edges(fx, lane)

    def gather2(m, k):
        block = F2.at[m, :, x]
        return remote(block, block, f2_s.at[m, k], f2_r.at[m, k], peers[k])

    halos2 = send_edges(GT2, H2, g_s, g_r)

    @pl.loop(0, FIELDS)
    def _(m):
        for k in range(3):
            gather2(m, k).start()

    @pl.loop(0, 128 // TILE)
    def _(t):
        r = pl.multiple_of(t * TILE, TILE)
        rows = pl.ds(r, TILE)
        src = source([U[m, rows, :] for m in range(FIELDS)], wall_of(r))
        for m in range(FIELDS):
            two = R[m, rows, :] - stencil(FX[m, rows, :])
            R[m, rows, :] = 0.5 * (two if src[m] is None else two + src[m])

    def share2(m):
        return remote(ps2.at[m], pr2.at[m], p2_s.at[m], p2_r.at[m], sibling)

    def give(m):
        return remote(zs.at[m], par.at[m], o_s.at[m], o_r.at[m], partner)

    def front(m):
        for k in range(3):
            gather2(m, k).wait_recv()
        total = jnp.dot(D[...], F2[m].reshape(512, COLS), preferred_element_type=jnp.float32)
        ps2[m] = total[128:]
        acc[m, pl.ds(0, 128)] = total[:128]
        share2(m).start()

    def back(m):
        share2(m).wait_recv()

        def value(first_row):
            rows = pl.ds(first_row, ROWS)
            edge = spread(TT[rows, :], m, wide)
            return R[m, rows, :] - edge - 0.5 * (acc[m, rows, :] + pr2[m, rows, :])

        zs[m] = value(pbase).astype(jnp.bfloat16)
        give(m).start()
        OUT[m, :, pl.ds(mine, COLS)] = value(base)

    wide = lax.broadcasted_iota(jnp.int32, (ROWS, COLS), 1)

    @pl.loop(0, LEAD)
    def _(m):
        front(m)

    receive_edges(halos2, H2)

    @pl.loop(0, 128 // TILE)
    def _(t):
        rows = pl.ds(pl.multiple_of(t * TILE, TILE), TILE)
        TT[rows, :] = 0.5 * mend(TT[rows, :] - G[rows, :], lane)

    @pl.loop(0, LEAD - 1)
    def _(m):
        back(m)

    @pl.loop(LEAD, FIELDS)
    def _(m):
        front(m)
        back(m - 1)

    back(FIELDS - 1)

    @pl.loop(0, FIELDS)
    def _(m):
        give(m).wait_recv()
        OUT[m, :, pl.ds(other, COLS)] = par[m].astype(jnp.float32)

    for copy in halos1 + halos2:
        copy.wait_send()
    for k in range(3):
        gather_own(k).wait_send()

    @pl.loop(0, PARTS)
    def _(t):
        swap(t).wait_send()
        for k in range(3):
            gather_part(t, k).wait_send()

    @pl.loop(0, FIELDS)
    def _(m):
        share1(m).wait_send()
        share2(m).wait_send()
        for k in range(3):
            gather2(m, k).wait_send()
        give(m).wait_send()


def on_device(mass_per_volume, motion_speed, agitation_energy, shear_deviatoric, thermal_current_array):
    def moved(a):
        return jnp.transpose(a, (1, 0, 2))

    full = (FIELDS, 128, COLS)
    gathered = (FIELDS, 2, 4, ROWS, COLS)
    dma = pltpu.SemaphoreType.DMA
    f32, bf16 = jnp.float32, jnp.bfloat16
    out = pl.pallas_call(
        kernel,
        out_shape=jax.ShapeDtypeStruct((FIELDS, ROWS, 2 * COLS), f32),
        in_specs=[pl.BlockSpec(memory_space=pltpu.HBM)] * 5,
        out_specs=pl.BlockSpec(memory_space=pltpu.VMEM),
        scratch_shapes=[
            pltpu.VMEM((FIELDS, ROWS, COLS), bf16),
            pltpu.VMEM(full, f32),
            pltpu.VMEM(full, f32),
            pltpu.VMEM(full, f32),
            pltpu.VMEM(gathered, bf16),
            pltpu.VMEM(gathered, bf16),
            pltpu.VMEM((FIELDS, ROWS, COLS), bf16),
            pltpu.VMEM((FIELDS, ROWS, COLS), bf16),
            pltpu.VMEM((FIELDS, 256, COLS), f32),
            pltpu.VMEM(full, f32),
            pltpu.VMEM(full, f32),
            pltpu.VMEM(full, f32),
            pltpu.VMEM(full, f32),
            pltpu.VMEM((256, 512), bf16),
            pltpu.VMEM((128, COLS), f32),
            pltpu.VMEM((COLS, 128), f32),
            pltpu.VMEM((COLS, 128), f32),
            pltpu.VMEM((2, 40, 128), f32),
            pltpu.VMEM((2, 40, 128), f32),
            pltpu.VMEM((128, 128), f32),
            pltpu.VMEM((2, FIELDS, ROWS, COLS), f32),
            pltpu.VMEM((FIELDS, ROWS, COLS), bf16),
            dma((2, 5)),
            dma((PARTS,)),
            dma((PARTS,)),
            dma((PARTS + 1, 3)),
            dma((PARTS + 1, 3)),
            dma((2,)),
            dma((2,)),
            dma((FIELDS,)),
            dma((FIELDS,)),
            dma((FIELDS, 3)),
            dma((FIELDS, 3)),
            dma((2,)),
            dma((2,)),
            dma((FIELDS,)),
            dma((FIELDS,)),
            dma((FIELDS,)),
            dma((FIELDS,)),
        ],
        compiler_params=pltpu.CompilerParams(
            collective_id=0, has_side_effects=True, vmem_limit_bytes=52_000_000
        ),
        name="sections",
    )(
        *(
            pltpu.with_memory_space_constraint(a, pltpu.HBM)
            for a in (
                mass_per_volume,
                moved(motion_speed),
                agitation_energy,
                moved(shear_deviatoric),
                moved(thermal_current_array),
            )
        )
    )
    return jnp.transpose(out, (1, 0, 2))


def solution(mesh):
    return jax.shard_map(
        on_device,
        mesh=mesh,
        in_specs=(
            P("gy", "gx"),
            P("gy", None, "gx"),
            P("gy", "gx"),
            P("gy", None, "gx"),
            P("gy", None, "gx"),
        ),
        out_specs=P("gy", None, "gx"),
        check_vma=False,
    )
```

```python
import math

import jax
import jax.numpy as jnp
from jax import lax
from jax.experimental import pallas as pl
from jax.experimental.pallas import tpu as pltpu
from jax.sharding import PartitionSpec as P

CROSS_NODES = 1024
LAST = CROSS_NODES - 1
HALF = math.pi / (2.0 * LAST)
MESH = pl.DeviceIdType.MESH

time_step = 0.05
enforcement_weight = 4.0
plate_speed = 0.5
dissipation_speed = 0.25
coeffs = (0.75, -0.15, 1.0 / 60.0)

FIELDS = 13
ROWS = 64
COLS = 128
TILE = 16
PARTS = ROWS // TILE
LEAD = 2

SPREAD = [(160.0, 1.25)] + [(40.0, 0.0)] * 3 + [(160.0, 1.25)] + [(50.0, 0.0)] * 8


def encode(value, field):
    rate, centre = SPREAD[field]
    return jnp.exp2(rate * (value - centre)).astype(jnp.bfloat16)


def decode(code, field):
    rate, centre = SPREAD[field]
    return jnp.log(code.astype(jnp.float32)) * (1.0 / (rate * math.log(2.0))) + centre


def flux(u, d):
    temp = u[4]
    speed = u[1:4]
    s = [[u[5], u[6], u[8]], [u[6], u[7], u[9]], [u[8], u[9], -(u[5] + u[7])]]
    q = u[10:13]
    carry = speed[d]
    out = [u[0] * carry]
    for i in range(3):
        term = speed[i] * carry + s[i][d]
        out.append(term + temp if i == d else term)
    out.append(carry * temp + (2.0 / 3.0) * q[d])
    for i, j in ((0, 0), (0, 1), (1, 1), (0, 2), (1, 2)):
        term = carry * s[i][j]
        if i == d and j == d:
            term = term + 0.8 * q[d]
        elif j == d:
            term = term + 0.4 * q[i]
        elif i == d:
            term = term + 0.4 * q[j]
        if i == j:
            term = term - (4.0 / 15.0) * q[d]
        out.append(term)
    for i in range(3):
        term = carry * q[i] + temp * s[i][d]
        out.append(term + 2.5 * temp * temp if i == d else term)
    return out


def source(u, wall):
    rate = u[0] * jnp.sqrt(u[4] * u[4] + 0.25)
    near = jnp.abs(wall)
    out = [None, -enforcement_weight * near * (u[1] - plate_speed * wall), None, None]
    out.append(-dissipation_speed * rate * u[4] - enforcement_weight * near * (u[4] - 1.0))
    out += [-0.8 * rate * u[k] for k in range(5, 10)]
    out += [-0.55 * rate * u[k] for k in range(10, 13)]
    return out


def stencil(f):
    total = None
    for k in range(3):
        term = coeffs[k] * (pltpu.roll(f, COLS - k - 1, 1) - pltpu.roll(f, k + 1, 1))
        total = term if total is None else total + term
    return total


def edges(f, lane):
    out = jnp.zeros_like(f[0])
    for m in range(FIELDS):
        moved = pltpu.roll(f[m], 6 * m + 3, 1)
        out = jnp.where((lane >= 6 * m) & (lane < 6 * m + 6), moved, out)
    return out


def mend(diff, lane):
    place = lane % 6
    a1, a2, a3 = coeffs
    right = a3 * pltpu.roll(diff, COLS - 3, 1)
    right += jnp.where(place >= 1, a2, 0.0) * pltpu.roll(diff, COLS - 2, 1)
    right += jnp.where(place >= 2, a1, 0.0) * pltpu.roll(diff, COLS - 1, 1)
    left = a3 * pltpu.roll(diff, 3, 1)
    left += jnp.where(place <= 4, a2, 0.0) * pltpu.roll(diff, 2, 1)
    left += jnp.where(place <= 3, a1, 0.0) * pltpu.roll(diff, 1, 1)
    return jnp.where(place < 3, right, -left)


def spread(packed, m, lane):
    return jnp.where((lane >= 125) | (lane < 3), pltpu.roll(packed, 125 - 6 * m, 1), 0.0)


def sine(x):
    z = x * x
    poly = 1.0 / 6227020800.0
    for c in (-1.0 / 39916800.0, 1.0 / 362880.0, -1.0 / 5040.0, 1.0 / 120.0, -1.0 / 6.0):
        poly = poly * z + c
    return x + x * z * poly


def grid_block(i, j):
    summed = i + j
    summed = jnp.minimum(summed, 2 * LAST - summed).astype(jnp.float32)
    differ = (i - j).astype(jnp.float32)
    same = i == j
    denom = -2.0 * sine(HALF * summed) * sine(HALF * differ)
    safe = jnp.where(same, 1.0, denom)

    def edge(index):
        return (index == 0) | (index == LAST)

    ratio = jnp.where(edge(i), 2.0, 1.0) * jnp.where(edge(j), 0.5, 1.0)
    ratio = jnp.where((i + j) % 2 == 0, ratio, -ratio)
    wave = sine(HALF * jnp.minimum(2 * i, 2 * (LAST - i)).astype(jnp.float32))
    off = (math.pi / LAST) * wave * ratio / safe
    tall = jnp.where(edge(i), 1.0, wave)
    diagonal = -HALF * sine(HALF * (LAST - 2 * i).astype(jnp.float32)) / tall
    return jnp.where(same, jnp.where(edge(i), 0.0, diagonal), off).astype(jnp.bfloat16)


def kernel(
    rho_ref,
    speed_ref,
    temp_ref,
    shear_ref,
    heat_ref,
    OUT,
    par,
    U,
    FX,
    R,
    F1,
    F2,
    enc,
    encr,
    acc,
    ps1,
    pr1,
    ps2,
    pr2,
    D,
    G,
    GT1,
    GT2,
    H1,
    H2,
    TT,
    X,
    zs,
    in_s,
    z_s,
    z_r,
    a_s,
    a_r,
    h_s,
    h_r,
    p1_s,
    p1_r,
    f2_s,
    f2_r,
    g_s,
    g_r,
    p2_s,
    p2_r,
    o_s,
    o_r,
):
    gx = lax.axis_index("gx")
    gy = lax.axis_index("gy")
    gxn = lax.axis_size("gx")
    x = gy // 4
    s = (gy // 2) % 2
    c = gy % 2

    def at(dgx, xx, ss, cc):
        return ((gx + dgx + gxn) % gxn, xx * 4 + ss * 2 + cc)

    partner = at(0, x, 1 - s, c)
    sibling = at(0, x, s, 1 - c)
    peers = [at(0, (x + k) % 4, s, c) for k in (1, 2, 3)]
    left_to = at(s - 1, x, 1 - s, c)
    right_to = at(s, x, 1 - s, c)

    barrier = pltpu.get_barrier_semaphore()
    greet = [partner, sibling, *peers, at(2 * s - 1, x, 1 - s, c)]
    for who in greet:
        pl.semaphore_signal(barrier, inc=1, device_id=who, device_id_type=MESH)

    mine = pl.multiple_of(s * COLS, COLS)
    other = pl.multiple_of((1 - s) * COLS, COLS)
    base = pl.multiple_of(s * ROWS, ROWS)
    pbase = pl.multiple_of((1 - s) * ROWS, ROWS)
    lane = lax.broadcasted_iota(jnp.int32, (TILE, COLS), 1)

    def remote(src, dst, ssem, rsem, who):
        return pltpu.make_async_remote_copy(
            src_ref=src, dst_ref=dst, send_sem=ssem, recv_sem=rsem, device_id=who, device_id_type=MESH
        )

    def load(half, column):
        cols = pl.ds(column, COLS)
        groups = ((rho_ref, 0, 0), (speed_ref, 1, 3), (temp_ref, 4, 0), (shear_ref, 5, 5), (heat_ref, 10, 3))
        copies = []
        for n, (ref, start, count) in enumerate(groups):
            src = ref.at[:, :, cols] if count else ref.at[:, cols]
            dst = X.at[half, pl.ds(start, count)] if count else X.at[half, start]
            copies.append(pltpu.make_async_copy(src, dst, in_s.at[half, n]))
        return copies

    loads = [load(0, other), load(1, mine)]
    for copy in loads[0] + loads[1]:
        copy.start()

    def inputs(half, r):
        return [X[half, m, pl.ds(r, TILE), :] for m in range(FIELDS)]

    def wall_of(r):
        k = r + lax.broadcasted_iota(jnp.int32, (TILE, COLS), 0)
        row = x * 256 + (r // ROWS) * 128 + c * ROWS + (k - (r // ROWS) * ROWS)
        return jnp.where(row == 0, 1.0, jnp.where(row == LAST, -1.0, 0.0))

    for copy in loads[0]:
        copy.wait()

    @pl.loop(0, ROWS // TILE)
    def _(t):
        r = pl.multiple_of(t * TILE, TILE)
        u = inputs(0, r)
        for m in range(FIELDS):
            enc[m, pl.ds(r, TILE), :] = encode(u[m], m)

    pl.semaphore_wait(barrier, len(greet))

    def swap(t):
        rows = pl.ds(pl.multiple_of(t * TILE, TILE), TILE)
        return remote(enc.at[:, rows], encr.at[:, rows], z_s.at[t], z_r.at[t], partner)

    for t in range(PARTS):
        swap(t).start()

    def across_flux(F, u, side, k):
        fy = flux(u, 1)
        for m in range(FIELDS):
            F[m, side, x, pl.ds(k, TILE), :] = fy[m].astype(jnp.bfloat16)

    def first(r, u):
        rows = pl.ds(r, TILE)
        for m in range(FIELDS):
            U[m, rows, :] = u[m]
        fx = flux(u, 0)
        G[rows, :] = edges(fx, lane)
        src = source(u, wall_of(r))
        for m in range(FIELDS):
            along = stencil(fx[m])
            R[m, rows, :] = -along if src[m] is None else src[m] - along

    for copy in loads[1]:
        copy.wait()

    @pl.loop(0, ROWS // TILE)
    def _(t):
        r = pl.multiple_of(t * TILE, TILE)
        u = inputs(1, r)
        across_flux(F1, u, s, r)
        first(pl.multiple_of(base + r, TILE), u)

    def gather_own(k):
        block = F1.at[:, s, x]
        return remote(block, block, a_s.at[PARTS, k], a_r.at[PARTS, k], peers[k])

    def gather_part(t, k):
        block = F1.at[:, 1 - s, x, pl.ds(pl.multiple_of(t * TILE, TILE), TILE)]
        return remote(block, block, a_s.at[t, k], a_r.at[t, k], peers[k])

    for k in range(3):
        gather_own(k).start()

    @pl.loop(0, 256 // TILE)
    def _(t):
        p = pl.multiple_of(t * TILE, TILE)
        row = p + lax.broadcasted_iota(jnp.int32, (TILE, 512), 0)
        rr = row % 128
        core = jnp.where(row < 128, c, 1 - c)
        i = x * 256 + (rr // ROWS) * 128 + core * ROWS + rr % ROWS
        col = lax.broadcasted_iota(jnp.int32, (TILE, 512), 1)
        j = ((col % 256) // ROWS) * 256 + (col // 256) * 128 + c * ROWS + col % ROWS
        D[pl.ds(p, TILE), :] = grid_block(i, j)

    for k in range(3):
        gather_own(k).wait_recv()

    def product(side, fields):
        columns = pl.ds(pl.multiple_of(side * 256, 256), 256)
        blocks = [F1[m, side].reshape(256, COLS) for m in fields]
        block = jnp.concatenate(blocks, axis=1) if len(blocks) > 1 else blocks[0]
        total = jnp.dot(D[:, columns], block, preferred_element_type=jnp.float32)
        return [total[:, n * COLS : (n + 1) * COLS] for n in range(len(blocks))]

    def in_pairs(body):
        @pl.loop(0, FIELDS // 2)
        def _(p):
            body((2 * p, 2 * p + 1))

        body((FIELDS - 1,))

    def own_side(fields):
        for m, total in zip(fields, product(s, fields)):
            acc[m] = total

    in_pairs(own_side)

    @pl.loop(0, PARTS)
    def _(t):
        swap(t).wait_recv()
        r = pl.multiple_of(t * TILE, TILE)
        u = [decode(encr[m, pl.ds(r, TILE), :], m) for m in range(FIELDS)]
        across_flux(F1, u, 1 - s, r)
        for k in range(3):
            gather_part(t, k).start()
        first(pl.multiple_of(pbase + r, TILE), u)

    packed = pl.ds(0, 80)

    def send_edges(GT, H, ssem, rsem):
        GT[...] = G[...].T.astype(jnp.bfloat16)
        copies = [
            remote(GT.at[packed], H.at[0], ssem.at[0], rsem.at[0], left_to),
            remote(GT.at[packed], H.at[1], ssem.at[1], rsem.at[1], right_to),
        ]
        for copy in copies:
            copy.start()
        return copies

    halos1 = send_edges(GT1, H1, h_s, h_r)

    @pl.loop(0, PARTS)
    def _(t):
        for k in range(3):
            gather_part(t, k).wait_recv()

    def share1(m):
        return remote(ps1.at[m], pr1.at[m], p1_s.at[m], p1_r.at[m], sibling)

    def other_side(fields):
        for m, total in zip(fields, product(1 - s, fields)):
            ps1[m] = acc[m, pl.ds(128, 128)] + total[128:]
            share1(m).start()
            acc[m, pl.ds(0, 128)] += total[:128]

    in_pairs(other_side)

    def receive_edges(copies, H):
        for copy in copies:
            copy.wait_recv()
        place = lax.broadcasted_iota(jnp.int32, (80, 128), 0) % 6
        TT[packed, :] = jnp.where(place >= 3, H[0].astype(jnp.float32), H[1].astype(jnp.float32))
        TT[pl.ds(80, 48), :] = jnp.zeros((48, COLS), jnp.float32)
        TT[...] = TT[...].T

    receive_edges(halos1, H1)

    @pl.loop(0, FIELDS)
    def _(m):
        share1(m).wait_recv()

    @pl.loop(0, 128 // TILE)
    def _(t):
        r = pl.multiple_of(t * TILE, TILE)
        rows = pl.ds(r, TILE)
        edge = mend(TT[rows, :] - G[rows, :], lane)
        u = []
        for m in range(FIELDS):
            one = R[m, rows, :] - spread(edge, m, lane) - (acc[m, rows, :] + pr1[m, rows, :])
            R[m, rows, :] = one
            u.append(U[m, rows, :] + time_step * one)
            U[m, rows, :] = u[m]
        side = r // ROWS
        across_flux(F2, u, side, pl.multiple_of(r - side * ROWS, TILE))
        fx = flux(u, 0)
        for m in range(FIELDS):
            FX[m, rows, :] = fx[m]
        G[rows, :] = edges(fx, lane)

    def gather2(m, k):
        block = F2.at[m, :, x]
        return remote(block, block, f2_s.at[m, k], f2_r.at[m, k], peers[k])

    halos2 = send_edges(GT2, H2, g_s, g_r)

    @pl.loop(0, FIELDS)
    def _(m):
        for k in range(3):
            gather2(m, k).start()

    @pl.loop(0, 128 // TILE)
    def _(t):
        r = pl.multiple_of(t * TILE, TILE)
        rows = pl.ds(r, TILE)
        src = source([U[m, rows, :] for m in range(FIELDS)], wall_of(r))
        for m in range(FIELDS):
            two = R[m, rows, :] - stencil(FX[m, rows, :])
            R[m, rows, :] = 0.5 * (two if src[m] is None else two + src[m])

    def share2(m):
        return remote(ps2.at[m], pr2.at[m], p2_s.at[m], p2_r.at[m], sibling)

    def give(m):
        return remote(zs.at[m], par.at[m], o_s.at[m], o_r.at[m], partner)

    def front(m):
        for k in range(3):
            gather2(m, k).wait_recv()
        total = jnp.dot(D[...], F2[m].reshape(512, COLS), preferred_element_type=jnp.float32)
        ps2[m] = total[128:]
        acc[m, pl.ds(0, 128)] = total[:128]
        share2(m).start()

    def back(m):
        share2(m).wait_recv()

        def value(first_row):
            rows = pl.ds(first_row, ROWS)
            edge = spread(TT[rows, :], m, wide)
            return R[m, rows, :] - edge - 0.5 * (acc[m, rows, :] + pr2[m, rows, :])

        zs[m] = value(pbase).astype(jnp.bfloat16)
        give(m).start()
        OUT[m, :, pl.ds(mine, COLS)] = value(base)

    wide = lax.broadcasted_iota(jnp.int32, (ROWS, COLS), 1)

    @pl.loop(0, LEAD)
    def _(m):
        front(m)

    receive_edges(halos2, H2)

    @pl.loop(0, 128 // TILE)
    def _(t):
        rows = pl.ds(pl.multiple_of(t * TILE, TILE), TILE)
        TT[rows, :] = 0.5 * mend(TT[rows, :] - G[rows, :], lane)

    @pl.loop(0, LEAD - 1)
    def _(m):
        back(m)

    @pl.loop(LEAD, FIELDS)
    def _(m):
        front(m)
        back(m - 1)

    back(FIELDS - 1)

    @pl.loop(0, FIELDS)
    def _(m):
        give(m).wait_recv()
        OUT[m, :, pl.ds(other, COLS)] = par[m].astype(jnp.float32)

    for copy in halos1 + halos2:
        copy.wait_send()
    for k in range(3):
        gather_own(k).wait_send()

    @pl.loop(0, PARTS)
    def _(t):
        swap(t).wait_send()
        for k in range(3):
            gather_part(t, k).wait_send()

    @pl.loop(0, FIELDS)
    def _(m):
        share1(m).wait_send()
        share2(m).wait_send()
        for k in range(3):
            gather2(m, k).wait_send()
        give(m).wait_send()


def on_device(mass_per_volume, motion_speed, agitation_energy, shear_deviatoric, thermal_current_array):
    def moved(a):
        return jnp.transpose(a, (1, 0, 2))

    full = (FIELDS, 128, COLS)
    gathered = (FIELDS, 2, 4, ROWS, COLS)
    dma = pltpu.SemaphoreType.DMA
    f32, bf16 = jnp.float32, jnp.bfloat16
    out = pl.pallas_call(
        kernel,
        out_shape=jax.ShapeDtypeStruct((FIELDS, ROWS, 2 * COLS), f32),
        in_specs=[pl.BlockSpec(memory_space=pltpu.HBM)] * 5,
        out_specs=pl.BlockSpec(memory_space=pltpu.VMEM),
        scratch_shapes=[
            pltpu.VMEM((FIELDS, ROWS, COLS), bf16),
            pltpu.VMEM(full, f32),
            pltpu.VMEM(full, f32),
            pltpu.VMEM(full, f32),
            pltpu.VMEM(gathered, bf16),
            pltpu.VMEM(gathered, bf16),
            pltpu.VMEM((FIELDS, ROWS, COLS), bf16),
            pltpu.VMEM((FIELDS, ROWS, COLS), bf16),
            pltpu.VMEM((FIELDS, 256, COLS), f32),
            pltpu.VMEM(full, f32),
            pltpu.VMEM(full, f32),
            pltpu.VMEM(full, f32),
            pltpu.VMEM(full, f32),
            pltpu.VMEM((256, 512), bf16),
            pltpu.VMEM((128, COLS), f32),
            pltpu.VMEM((COLS, 128), bf16),
            pltpu.VMEM((COLS, 128), bf16),
            pltpu.VMEM((2, 80, 128), bf16),
            pltpu.VMEM((2, 80, 128), bf16),
            pltpu.VMEM((128, 128), f32),
            pltpu.VMEM((2, FIELDS, ROWS, COLS), f32),
            pltpu.VMEM((FIELDS, ROWS, COLS), bf16),
            dma((2, 5)),
            dma((PARTS,)),
            dma((PARTS,)),
            dma((PARTS + 1, 3)),
            dma((PARTS + 1, 3)),
            dma((2,)),
            dma((2,)),
            dma((FIELDS,)),
            dma((FIELDS,)),
            dma((FIELDS, 3)),
            dma((FIELDS, 3)),
            dma((2,)),
            dma((2,)),
            dma((FIELDS,)),
            dma((FIELDS,)),
            dma((FIELDS,)),
            dma((FIELDS,)),
        ],
        compiler_params=pltpu.CompilerParams(
            collective_id=0, has_side_effects=True, vmem_limit_bytes=52_000_000
        ),
        name="sections",
    )(
        *(
            pltpu.with_memory_space_constraint(a, pltpu.HBM)
            for a in (
                mass_per_volume,
                moved(motion_speed),
                agitation_energy,
                moved(shear_deviatoric),
                moved(thermal_current_array),
            )
        )
    )
    return jnp.transpose(out, (1, 0, 2))


def solution(mesh):
    return jax.shard_map(
        on_device,
        mesh=mesh,
        in_specs=(
            P("gy", "gx"),
            P("gy", None, "gx"),
            P("gy", "gx"),
            P("gy", None, "gx"),
            P("gy", None, "gx"),
        ),
        out_specs=P("gy", None, "gx"),
        check_vma=False,
    )
```

```python
import math

import jax
import jax.numpy as jnp
from jax import lax
from jax.experimental import pallas as pl
from jax.experimental.pallas import tpu as pltpu
from jax.sharding import PartitionSpec as P

CROSS_NODES = 1024
LAST = CROSS_NODES - 1
HALF = math.pi / (2.0 * LAST)
MESH = pl.DeviceIdType.MESH

time_step = 0.05
enforcement_weight = 4.0
plate_speed = 0.5
dissipation_speed = 0.25
coeffs = (0.75, -0.15, 1.0 / 60.0)

FIELDS = 13
ROWS = 64
COLS = 128
TILE = 16
PARTS = ROWS // TILE
LEAD = 2

SPREAD = [(160.0, 1.25)] + [(40.0, 0.0)] * 3 + [(160.0, 1.25)] + [(50.0, 0.0)] * 8


def encode(value, field):
    rate, centre = SPREAD[field]
    return jnp.exp2(rate * (value - centre)).astype(jnp.bfloat16)


def decode(code, field):
    rate, centre = SPREAD[field]
    return jnp.log(code.astype(jnp.float32)) * (1.0 / (rate * math.log(2.0))) + centre


def flux(u, d):
    temp = u[4]
    speed = u[1:4]
    s = [[u[5], u[6], u[8]], [u[6], u[7], u[9]], [u[8], u[9], -(u[5] + u[7])]]
    q = u[10:13]
    carry = speed[d]
    out = [u[0] * carry]
    for i in range(3):
        term = speed[i] * carry + s[i][d]
        out.append(term + temp if i == d else term)
    out.append(carry * temp + (2.0 / 3.0) * q[d])
    for i, j in ((0, 0), (0, 1), (1, 1), (0, 2), (1, 2)):
        term = carry * s[i][j]
        if i == d and j == d:
            term = term + 0.8 * q[d]
        elif j == d:
            term = term + 0.4 * q[i]
        elif i == d:
            term = term + 0.4 * q[j]
        if i == j:
            term = term - (4.0 / 15.0) * q[d]
        out.append(term)
    for i in range(3):
        term = carry * q[i] + temp * s[i][d]
        out.append(term + 2.5 * temp * temp if i == d else term)
    return out


def source(u, wall):
    rate = u[0] * jnp.sqrt(u[4] * u[4] + 0.25)
    near = jnp.abs(wall)
    out = [None, -enforcement_weight * near * (u[1] - plate_speed * wall), None, None]
    out.append(-dissipation_speed * rate * u[4] - enforcement_weight * near * (u[4] - 1.0))
    out += [-0.8 * rate * u[k] for k in range(5, 10)]
    out += [-0.55 * rate * u[k] for k in range(10, 13)]
    return out


def stencil(f):
    total = None
    for k in range(3):
        term = coeffs[k] * (pltpu.roll(f, COLS - k - 1, 1) - pltpu.roll(f, k + 1, 1))
        total = term if total is None else total + term
    return total


def edges(f, lane):
    out = jnp.zeros_like(f[0])
    for m in range(FIELDS):
        moved = pltpu.roll(f[m], 6 * m + 3, 1)
        out = jnp.where((lane >= 6 * m) & (lane < 6 * m + 6), moved, out)
    return out


def mend(diff, lane):
    place = lane % 6
    a1, a2, a3 = coeffs
    right = a3 * pltpu.roll(diff, COLS - 3, 1)
    right += jnp.where(place >= 1, a2, 0.0) * pltpu.roll(diff, COLS - 2, 1)
    right += jnp.where(place >= 2, a1, 0.0) * pltpu.roll(diff, COLS - 1, 1)
    left = a3 * pltpu.roll(diff, 3, 1)
    left += jnp.where(place <= 4, a2, 0.0) * pltpu.roll(diff, 2, 1)
    left += jnp.where(place <= 3, a1, 0.0) * pltpu.roll(diff, 1, 1)
    return jnp.where(place < 3, right, -left)


def spread(packed, m, lane):
    return jnp.where((lane >= 125) | (lane < 3), pltpu.roll(packed, 125 - 6 * m, 1), 0.0)


def sine(x):
    z = x * x
    poly = 1.0 / 6227020800.0
    for c in (-1.0 / 39916800.0, 1.0 / 362880.0, -1.0 / 5040.0, 1.0 / 120.0, -1.0 / 6.0):
        poly = poly * z + c
    return x + x * z * poly


def grid_block(i, j):
    summed = i + j
    summed = jnp.minimum(summed, 2 * LAST - summed).astype(jnp.float32)
    differ = (i - j).astype(jnp.float32)
    same = i == j
    denom = -2.0 * sine(HALF * summed) * sine(HALF * differ)
    safe = jnp.where(same, 1.0, denom)

    def edge(index):
        return (index == 0) | (index == LAST)

    ratio = jnp.where(edge(i), 2.0, 1.0) * jnp.where(edge(j), 0.5, 1.0)
    ratio = jnp.where((i + j) % 2 == 0, ratio, -ratio)
    wave = sine(HALF * jnp.minimum(2 * i, 2 * (LAST - i)).astype(jnp.float32))
    off = (math.pi / LAST) * wave * ratio / safe
    tall = jnp.where(edge(i), 1.0, wave)
    diagonal = -HALF * sine(HALF * (LAST - 2 * i).astype(jnp.float32)) / tall
    return jnp.where(same, jnp.where(edge(i), 0.0, diagonal), off).astype(jnp.bfloat16)


def kernel(
    rho_ref,
    speed_ref,
    temp_ref,
    shear_ref,
    heat_ref,
    OUT,
    par,
    U,
    FX,
    R,
    F1,
    F2,
    enc,
    encr,
    acc,
    ps1,
    pr1,
    ps2,
    pr2,
    D,
    G,
    GT1,
    GT2,
    H1,
    H2,
    TT,
    X,
    zs,
    in_s,
    z_s,
    z_r,
    a_s,
    a_r,
    h_s,
    h_r,
    p1_s,
    p1_r,
    f2_s,
    f2_r,
    g_s,
    g_r,
    p2_s,
    p2_r,
    o_s,
    o_r,
):
    gx = lax.axis_index("gx")
    gy = lax.axis_index("gy")
    gxn = lax.axis_size("gx")
    x = gy // 4
    s = (gy // 2) % 2
    c = gy % 2

    def at(dgx, xx, ss, cc):
        return ((gx + dgx + gxn) % gxn, xx * 4 + ss * 2 + cc)

    partner = at(0, x, 1 - s, c)
    sibling = at(0, x, s, 1 - c)
    peers = [at(0, (x + k) % 4, s, c) for k in (1, 2, 3)]
    left_to = at(s - 1, x, 1 - s, c)
    right_to = at(s, x, 1 - s, c)

    barrier = pltpu.get_barrier_semaphore()
    greet = [partner, sibling, *peers, at(2 * s - 1, x, 1 - s, c)]
    for who in greet:
        pl.semaphore_signal(barrier, inc=1, device_id=who, device_id_type=MESH)

    mine = pl.multiple_of(s * COLS, COLS)
    other = pl.multiple_of((1 - s) * COLS, COLS)
    base = pl.multiple_of(s * ROWS, ROWS)
    pbase = pl.multiple_of((1 - s) * ROWS, ROWS)
    lane = lax.broadcasted_iota(jnp.int32, (TILE, COLS), 1)

    def remote(src, dst, ssem, rsem, who):
        return pltpu.make_async_remote_copy(
            src_ref=src, dst_ref=dst, send_sem=ssem, recv_sem=rsem, device_id=who, device_id_type=MESH
        )

    def load(half, column):
        cols = pl.ds(column, COLS)
        groups = ((rho_ref, 0, 0), (speed_ref, 1, 3), (temp_ref, 4, 0), (shear_ref, 5, 5), (heat_ref, 10, 3))
        copies = []
        for n, (ref, start, count) in enumerate(groups):
            src = ref.at[:, :, cols] if count else ref.at[:, cols]
            dst = X.at[half, pl.ds(start, count)] if count else X.at[half, start]
            copies.append(pltpu.make_async_copy(src, dst, in_s.at[half, n]))
        return copies

    loads = [load(0, other), load(1, mine)]
    for copy in loads[0] + loads[1]:
        copy.start()

    def inputs(half, r):
        return [X[half, m, pl.ds(r, TILE), :] for m in range(FIELDS)]

    def wall_of(r):
        k = r + lax.broadcasted_iota(jnp.int32, (TILE, COLS), 0)
        row = x * 256 + (r // ROWS) * 128 + c * ROWS + (k - (r // ROWS) * ROWS)
        return jnp.where(row == 0, 1.0, jnp.where(row == LAST, -1.0, 0.0))

    for copy in loads[0]:
        copy.wait()

    @pl.loop(0, ROWS // TILE)
    def _(t):
        r = pl.multiple_of(t * TILE, TILE)
        u = inputs(0, r)
        for m in range(FIELDS):
            enc[m, pl.ds(r, TILE), :] = encode(u[m], m)

    pl.semaphore_wait(barrier, len(greet))

    def swap(t):
        rows = pl.ds(pl.multiple_of(t * TILE, TILE), TILE)
        return remote(enc.at[:, rows], encr.at[:, rows], z_s.at[t], z_r.at[t], partner)

    for t in range(PARTS):
        swap(t).start()

    def across_flux(F, u, side, k):
        fy = flux(u, 1)
        for m in range(FIELDS):
            F[m, side, x, pl.ds(k, TILE), :] = fy[m].astype(jnp.bfloat16)

    def first(r, u):
        rows = pl.ds(r, TILE)
        for m in range(FIELDS):
            U[m, rows, :] = u[m]
        fx = flux(u, 0)
        G[rows, :] = edges(fx, lane)
        src = source(u, wall_of(r))
        for m in range(FIELDS):
            along = stencil(fx[m])
            R[m, rows, :] = -along if src[m] is None else src[m] - along

    for copy in loads[1]:
        copy.wait()

    @pl.loop(0, ROWS // TILE)
    def _(t):
        r = pl.multiple_of(t * TILE, TILE)
        u = inputs(1, r)
        across_flux(F1, u, s, r)
        first(pl.multiple_of(base + r, TILE), u)

    def gather_own(k):
        block = F1.at[:, s, x]
        return remote(block, block, a_s.at[PARTS, k], a_r.at[PARTS, k], peers[k])

    def gather_part(t, k):
        block = F1.at[:, 1 - s, x, pl.ds(pl.multiple_of(t * TILE, TILE), TILE)]
        return remote(block, block, a_s.at[t, k], a_r.at[t, k], peers[k])

    for k in range(3):
        gather_own(k).start()

    @pl.loop(0, 256 // TILE)
    def _(t):
        p = pl.multiple_of(t * TILE, TILE)
        row = p + lax.broadcasted_iota(jnp.int32, (TILE, 512), 0)
        rr = row % 128
        core = jnp.where(row < 128, c, 1 - c)
        i = x * 256 + (rr // ROWS) * 128 + core * ROWS + rr % ROWS
        col = lax.broadcasted_iota(jnp.int32, (TILE, 512), 1)
        j = ((col % 256) // ROWS) * 256 + (col // 256) * 128 + c * ROWS + col % ROWS
        D[pl.ds(p, TILE), :] = grid_block(i, j)

    for k in range(3):
        gather_own(k).wait_recv()

    def product(side, fields):
        columns = pl.ds(pl.multiple_of(side * 256, 256), 256)
        blocks = [F1[m, side].reshape(256, COLS) for m in fields]
        block = jnp.concatenate(blocks, axis=1) if len(blocks) > 1 else blocks[0]
        total = jnp.dot(D[:, columns], block, preferred_element_type=jnp.float32)
        return [total[:, n * COLS : (n + 1) * COLS] for n in range(len(blocks))]

    def in_pairs(body):
        @pl.loop(0, FIELDS // 2)
        def _(p):
            body((2 * p, 2 * p + 1))

        body((FIELDS - 1,))

    def own_side(fields):
        for m, total in zip(fields, product(s, fields)):
            acc[m] = total

    in_pairs(own_side)

    @pl.loop(0, PARTS)
    def _(t):
        swap(t).wait_recv()
        r = pl.multiple_of(t * TILE, TILE)
        u = [decode(encr[m, pl.ds(r, TILE), :], m) for m in range(FIELDS)]
        across_flux(F1, u, 1 - s, r)
        for k in range(3):
            gather_part(t, k).start()
        first(pl.multiple_of(pbase + r, TILE), u)

    packed = pl.ds(0, 80)

    def send_edges(GT, H, ssem, rsem):
        GT[...] = G[...].T.astype(jnp.bfloat16)
        copies = [
            remote(GT.at[packed], H.at[0], ssem.at[0], rsem.at[0], left_to),
            remote(GT.at[packed], H.at[1], ssem.at[1], rsem.at[1], right_to),
        ]
        for copy in copies:
            copy.start()
        return copies

    halos1 = send_edges(GT1, H1, h_s, h_r)

    @pl.loop(0, PARTS)
    def _(t):
        for k in range(3):
            gather_part(t, k).wait_recv()

    def share1(m):
        return remote(ps1.at[m], pr1.at[m], p1_s.at[m], p1_r.at[m], sibling)

    def other_side(fields):
        for m, total in zip(fields, product(1 - s, fields)):
            ps1[m] = acc[m, pl.ds(128, 128)] + total[128:]
            share1(m).start()
            acc[m, pl.ds(0, 128)] += total[:128]

    in_pairs(other_side)

    def receive_edges(copies, H):
        for copy in copies:
            copy.wait_recv()
        place = lax.broadcasted_iota(jnp.int32, (80, 128), 0) % 6
        TT[packed, :] = jnp.where(place >= 3, H[0].astype(jnp.float32), H[1].astype(jnp.float32))
        TT[pl.ds(80, 48), :] = jnp.zeros((48, COLS), jnp.float32)
        TT[...] = TT[...].T

    receive_edges(halos1, H1)

    @pl.loop(0, FIELDS)
    def _(m):
        share1(m).wait_recv()

    @pl.loop(0, 128 // TILE)
    def _(t):
        r = pl.multiple_of(t * TILE, TILE)
        rows = pl.ds(r, TILE)
        edge = mend(TT[rows, :] - G[rows, :], lane)
        u = []
        for m in range(FIELDS):
            one = R[m, rows, :] - spread(edge, m, lane) - (acc[m, rows, :] + pr1[m, rows, :])
            R[m, rows, :] = one
            u.append(U[m, rows, :] + time_step * one)
            U[m, rows, :] = u[m]
        side = r // ROWS
        across_flux(F2, u, side, pl.multiple_of(r - side * ROWS, TILE))
        fx = flux(u, 0)
        for m in range(FIELDS):
            FX[m, rows, :] = fx[m]
        G[rows, :] = edges(fx, lane)

    def gather2(m, k):
        block = F2.at[m, :, x]
        return remote(block, block, f2_s.at[m, k], f2_r.at[m, k], peers[k])

    @pl.loop(0, LEAD)
    def _(m):
        for k in range(3):
            gather2(m, k).start()

    halos2 = send_edges(GT2, H2, g_s, g_r)

    @pl.loop(LEAD, FIELDS)
    def _(m):
        for k in range(3):
            gather2(m, k).start()

    @pl.loop(0, 128 // TILE)
    def _(t):
        r = pl.multiple_of(t * TILE, TILE)
        rows = pl.ds(r, TILE)
        src = source([U[m, rows, :] for m in range(FIELDS)], wall_of(r))
        for m in range(FIELDS):
            two = R[m, rows, :] - stencil(FX[m, rows, :])
            R[m, rows, :] = 0.5 * (two if src[m] is None else two + src[m])

    def share2(m):
        return remote(ps2.at[m], pr2.at[m], p2_s.at[m], p2_r.at[m], sibling)

    def give(m):
        return remote(zs.at[m], par.at[m], o_s.at[m], o_r.at[m], partner)

    def front(m):
        for k in range(3):
            gather2(m, k).wait_recv()
        total = jnp.dot(D[...], F2[m].reshape(512, COLS), preferred_element_type=jnp.float32)
        ps2[m] = total[128:]
        acc[m, pl.ds(0, 128)] = total[:128]
        share2(m).start()

    def back(m):
        share2(m).wait_recv()

        def value(first_row):
            rows = pl.ds(first_row, ROWS)
            edge = spread(TT[rows, :], m, wide)
            return R[m, rows, :] - edge - 0.5 * (acc[m, rows, :] + pr2[m, rows, :])

        zs[m] = value(pbase).astype(jnp.bfloat16)
        give(m).start()
        OUT[m, :, pl.ds(mine, COLS)] = value(base)

    wide = lax.broadcasted_iota(jnp.int32, (ROWS, COLS), 1)

    @pl.loop(0, LEAD)
    def _(m):
        front(m)

    receive_edges(halos2, H2)

    @pl.loop(0, 128 // TILE)
    def _(t):
        rows = pl.ds(pl.multiple_of(t * TILE, TILE), TILE)
        TT[rows, :] = 0.5 * mend(TT[rows, :] - G[rows, :], lane)

    @pl.loop(0, LEAD - 1)
    def _(m):
        back(m)

    @pl.loop(LEAD, FIELDS)
    def _(m):
        front(m)
        back(m - 1)

    back(FIELDS - 1)

    @pl.loop(0, FIELDS)
    def _(m):
        give(m).wait_recv()
        OUT[m, :, pl.ds(other, COLS)] = par[m].astype(jnp.float32)

    for copy in halos1 + halos2:
        copy.wait_send()
    for k in range(3):
        gather_own(k).wait_send()

    @pl.loop(0, PARTS)
    def _(t):
        swap(t).wait_send()
        for k in range(3):
            gather_part(t, k).wait_send()

    @pl.loop(0, FIELDS)
    def _(m):
        share1(m).wait_send()
        share2(m).wait_send()
        for k in range(3):
            gather2(m, k).wait_send()
        give(m).wait_send()


def on_device(mass_per_volume, motion_speed, agitation_energy, shear_deviatoric, thermal_current_array):
    def moved(a):
        return jnp.transpose(a, (1, 0, 2))

    full = (FIELDS, 128, COLS)
    gathered = (FIELDS, 2, 4, ROWS, COLS)
    dma = pltpu.SemaphoreType.DMA
    f32, bf16 = jnp.float32, jnp.bfloat16
    out = pl.pallas_call(
        kernel,
        out_shape=jax.ShapeDtypeStruct((FIELDS, ROWS, 2 * COLS), f32),
        in_specs=[pl.BlockSpec(memory_space=pltpu.HBM)] * 5,
        out_specs=pl.BlockSpec(memory_space=pltpu.VMEM),
        scratch_shapes=[
            pltpu.VMEM((FIELDS, ROWS, COLS), bf16),
            pltpu.VMEM(full, f32),
            pltpu.VMEM(full, f32),
            pltpu.VMEM(full, f32),
            pltpu.VMEM(gathered, bf16),
            pltpu.VMEM(gathered, bf16),
            pltpu.VMEM((FIELDS, ROWS, COLS), bf16),
            pltpu.VMEM((FIELDS, ROWS, COLS), bf16),
            pltpu.VMEM((FIELDS, 256, COLS), f32),
            pltpu.VMEM(full, f32),
            pltpu.VMEM(full, f32),
            pltpu.VMEM(full, f32),
            pltpu.VMEM(full, f32),
            pltpu.VMEM((256, 512), bf16),
            pltpu.VMEM((128, COLS), f32),
            pltpu.VMEM((COLS, 128), bf16),
            pltpu.VMEM((COLS, 128), bf16),
            pltpu.VMEM((2, 80, 128), bf16),
            pltpu.VMEM((2, 80, 128), bf16),
            pltpu.VMEM((128, 128), f32),
            pltpu.VMEM((2, FIELDS, ROWS, COLS), f32),
            pltpu.VMEM((FIELDS, ROWS, COLS), bf16),
            dma((2, 5)),
            dma((PARTS,)),
            dma((PARTS,)),
            dma((PARTS + 1, 3)),
            dma((PARTS + 1, 3)),
            dma((2,)),
            dma((2,)),
            dma((FIELDS,)),
            dma((FIELDS,)),
            dma((FIELDS, 3)),
            dma((FIELDS, 3)),
            dma((2,)),
            dma((2,)),
            dma((FIELDS,)),
            dma((FIELDS,)),
            dma((FIELDS,)),
            dma((FIELDS,)),
        ],
        compiler_params=pltpu.CompilerParams(
            collective_id=0, has_side_effects=True, vmem_limit_bytes=52_000_000
        ),
        name="sections",
    )(
        *(
            pltpu.with_memory_space_constraint(a, pltpu.HBM)
            for a in (
                mass_per_volume,
                moved(motion_speed),
                agitation_energy,
                moved(shear_deviatoric),
                moved(thermal_current_array),
            )
        )
    )
    return jnp.transpose(out, (1, 0, 2))


def solution(mesh):
    return jax.shard_map(
        on_device,
        mesh=mesh,
        in_specs=(
            P("gy", "gx"),
            P("gy", None, "gx"),
            P("gy", "gx"),
            P("gy", None, "gx"),
            P("gy", None, "gx"),
        ),
        out_specs=P("gy", None, "gx"),
        check_vma=False,
    )
```
